1024 devices in a mesh: tm: 8 (over y), band: 8 (over z_hi, core), space: 16 (over z_lo, x).
Axes of the slice: x: 4, y: 8, z: 16 (z_hi: 4, z_lo: 4; z = z_hi * 4 + z_lo), core: 2. Of those that a mesh axis runs over, the one named last changes fastest.
Arguments:
- evecs: bfloat16 [8, 2, 3, 21504, 128], P(None, None, None, ('tm', 'space')), may hold values from -0.31640625 to 0.31640625
- peram: bfloat16 [8, 32, 2, 128, 128], P('tm'), may hold values from -0.375 to 0.375
- mom: int32 [8, 3], P('band'), may hold values from 1 to 2
- pairs: int32 [8, 6], P('band'), may hold values from 0 to 31, as said below
- counts: int32 [8], P('band'), may hold values from 2 to 6, as said below
Outputs:
- meson: float32 [8, 128, 8, 256], P('tm', 'space', 'band')
- blocks: float32 [8, 48, 128, 8, 256], P('tm', 'band', 'space')
The draws below stay inside these ranges and needn't reach their ends.
Inputs may be any that keep to these rules, and one draw needn't show every extreme that they name: `pairs`: in row b the slots 0 to counts[b] - 1 hold distinct blocks; the other slots hold 0. A block may stand in live slots of several rows. `counts`: the largest count is exactly 6.
All inputs are finite; a program needn't handle non-finite values.
Results may differ from the reference program's by a relative error of at most 0.004.
Values may be sent and summed in bfloat16 or wider, within the bound.
No kernel may reach another device: no remote copies, remote signals or barrier semaphores. Data moves between devices by JAX's collectives and lax.ppermute only.
A program may use at most 32 MiB of HBM per device.

```python
import math
import jax
import jax.numpy as jnp
from jax import lax

NEV = 128
EXTENT = 64
NBLK = 32
CAP = 6
SLOTS = 48
NT = 8
NMOM = 8
SITES = 21504
N_BAND = 8


def table_parts(key):
    inner = jax.random.fold_in(key, 7)
    first, second, third = jax.random.split(inner, 3)
    heavy = jax.random.randint(first, (), 0, N_BAND)
    bands = jnp.arange(N_BAND, dtype=jnp.int32)
    drawn = jax.random.randint(second, (N_BAND,), CAP // 3, CAP + 1)
    counts = jnp.where(bands == heavy, CAP, drawn).astype(jnp.int32)
    row_keys = jax.random.split(third, N_BAND)
    orders = jax.vmap(lambda k: jax.random.permutation(k, NBLK))(row_keys)[:, :CAP].astype(jnp.int32)
    slots = jnp.arange(CAP, dtype=jnp.int32)
    live = slots[None, :] < counts[:, None]
    pairs = jnp.where(live, orders, 0).astype(jnp.int32)
    return (pairs, counts)


def draw_pairs(key, part):
    return table_parts(key)[0]


def draw_counts(key, part):
    return table_parts(key)[1]


def set_ends(entries, own_key, low, high):
    longest = entries.shape.index(max(entries.shape))
    spots = []
    for shift in (0, 1):
        where = [jax.random.randint(jax.random.fold_in(own_key, axis), (), 0, length) for axis, length in enumerate(entries.shape)]
        where[longest] = (where[longest] + shift) % entries.shape[longest]
        spots.append(tuple(where))
    return entries.at[spots[0]].set(low).at[spots[1]].set(high)


def shard_levels(key, extent, cuts, low, high):
    def one(dim, blocks):
        heights = jax.random.uniform(jax.random.fold_in(jax.random.fold_in(key, 6), dim), (blocks,), jnp.float32, low / len(cuts), high / len(cuts))
        return jnp.repeat(jnp.exp(heights), extent[dim] // blocks).reshape((-1,) + (1,) * (len(extent) - dim - 1))

    level = one(*cuts[0])
    for cut in cuts[1:]:
        level = level * one(*cut)
    return level


def noise(key, dims, spread, most, cuts=(), held_as=jnp.bfloat16):
    entries = spread * jax.random.normal(key, dims, jnp.float32)
    if cuts:
        entries = entries * shard_levels(key, dims, cuts, -0.22, 0.18)
    return jnp.clip(entries, -most, most).astype(held_as)


def setup_inputs(seed: int = 0) -> dict:
    splits = jax.random.split(jax.random.key(seed), 6)
    evecs = noise(splits[0], (NT, 2, 3, SITES, NEV), ((6 * SITES) ** -0.25), 0.31640625, ((3, 128),))
    peram = noise(splits[1], (NT, NBLK, 2, NEV, NEV), (2 * NEV) ** -0.5, 0.375, ((0, 8),))
    mom = set_ends(jax.random.randint(splits[2], (NMOM, 3), 1, 3), jax.random.fold_in(splits[2], 1), 1, 2).astype(jnp.int32)
    pairs = draw_pairs(jax.random.fold_in(splits[5], 71), 0)
    counts = draw_counts(jax.random.fold_in(splits[5], 71), 0)
    return dict(evecs=evecs, peram=peram, mom=mom, pairs=pairs, counts=counts)


def site_phases(row, xs, ys, zs):
    wave = (row[0] * xs + row[1] * ys + row[2] * zs) % EXTENT
    theta = wave.astype(jnp.float32) * jnp.float32(2.0 * math.pi / EXTENT)
    return jnp.cos(theta), jnp.sin(theta)


def reference(evecs, peram, mom, pairs, counts):
    glob = jnp.arange(SITES, dtype=jnp.int32)
    xs = glob % EXTENT
    ys = (glob // EXTENT) % EXTENT
    zs = glob // (EXTENT * EXTENT)
    fields = []
    for tslice in range(NT):
        vreal = evecs[tslice, 0].astype(jnp.float32)
        vimag = evecs[tslice, 1].astype(jnp.float32)
        left = evecs[tslice].astype(jnp.float32).reshape(6 * SITES, NEV)

        def per_mom(row):
            cosine, sine = site_phases(row, xs, ys, zs)
            cosine = cosine[None, :, None]
            sine = sine[None, :, None]
            wreal = cosine * vreal + sine * vimag
            wimag = cosine * vimag - sine * vreal
            right = jnp.stack([jnp.concatenate([wreal, wimag], -1), jnp.concatenate([wimag, -wreal], -1)])
            right = lax.optimization_barrier(right.astype(jnp.bfloat16)).astype(jnp.float32)
            right = right.reshape(6 * SITES, 2 * NEV)
            return lax.dot_general(left, right, (((0,), (0,)), ((), ())), precision=lax.Precision.HIGHEST, preferred_element_type=jnp.float32)

        result = lax.map(per_mom, mom)
        fields.append(jnp.transpose(result, (1, 0, 2)))
    meson = jnp.stack(fields)
    half = lax.optimization_barrier(meson.astype(jnp.bfloat16)).astype(jnp.float32)
    live = (jnp.arange(CAP, dtype=jnp.int32)[None, :] < counts[:, None]).reshape(-1).astype(jnp.float32)
    flat_pairs = pairs.reshape(-1)
    outputs = []
    for tslice in range(NT):
        chosen = peram[tslice][flat_pairs].astype(jnp.float32)
        preal = chosen[:, 0]
        pimag = chosen[:, 1]
        right = jnp.concatenate([jnp.concatenate([preal, pimag], -1), jnp.concatenate([-pimag, preal], -1)], axis=1)
        left = half[tslice].reshape(NEV * NMOM, 2 * NEV)
        prod = jnp.einsum("rk,ckn->crn", left, right, precision=lax.Precision.HIGHEST, preferred_element_type=jnp.float32)
        prod = prod.reshape(SLOTS, NEV, NMOM, 2 * NEV) * live[:, None, None, None]
        outputs.append(prod)
    return meson, jnp.stack(outputs)
```

```python
import math

import jax
import jax.numpy as jnp
from jax import lax
from jax.experimental import pallas as pl
from jax.experimental.pallas import tpu as pltpu
from jax.sharding import PartitionSpec as P

EXTENT = 64


def gram_kernel(base_ref, mom_ref, pairs_ref, evecs_ref, peram_ref, out_ref, chosen_ref, cos_ref, sin_ref, sems):
    step = pl.program_id(0)
    slots = chosen_ref.shape[0]
    copies = [
        pltpu.make_async_copy(peram_ref.at[pairs_ref[0, c]], chosen_ref.at[c], sems.at[c])
        for c in range(slots)
    ]

    @pl.when(step == 0)
    def _():
        for copy in copies:
            copy.start()
        site = base_ref[0] + lax.broadcasted_iota(jnp.int32, cos_ref.shape, 0)
        xs = site & (EXTENT - 1)
        ys = (site >> 6) & (EXTENT - 1)
        zs = site >> 12
        wave = (mom_ref[0, 0] * xs + mom_ref[0, 1] * ys + mom_ref[0, 2] * zs) & (EXTENT - 1)
        theta = wave.astype(jnp.float32) * jnp.float32(2.0 * math.pi / EXTENT)
        cos_ref[...] = jnp.cos(theta)
        sin_ref[...] = jnp.sin(theta)

    cosine = cos_ref[...]
    sine = sin_ref[...]
    acc = jnp.zeros(out_ref.shape, jnp.float32)
    for colour in range(evecs_ref.shape[2]):
        real = evecs_ref[0, 0, colour]
        imag = evecs_ref[0, 1, colour]
        vreal = real.astype(jnp.float32)
        vimag = imag.astype(jnp.float32)
        wreal = cosine * vreal + sine * vimag
        wimag = cosine * vimag - sine * vreal
        wreal16 = wreal.astype(jnp.bfloat16)
        wimag16 = wimag.astype(jnp.bfloat16)
        upper = jnp.concatenate([wreal16, wimag16], axis=1)
        lower = jnp.concatenate([wimag16, -wreal16], axis=1)
        dims = (((0,), (0,)), ((), ()))
        acc += lax.dot_general(real, upper, dims, preferred_element_type=jnp.float32)
        acc += lax.dot_general(imag, lower, dims, preferred_element_type=jnp.float32)
    out_ref[...] = acc.astype(out_ref.dtype)

    @pl.when(step == pl.num_programs(0) - 1)
    def _():
        for copy in copies:
            copy.wait()


def sum_kernel(parts_ref, meson_ref, half_ref):
    total = jnp.sum(parts_ref[...].astype(jnp.float32), axis=0)
    half = total.astype(jnp.bfloat16)
    for row in range(total.shape[0]):
        meson_ref[row] = total[row : row + 1]
    for band in range(half_ref.shape[0]):
        half_ref[band] = half


def block_kernel(counts_ref, half_ref, chosen_ref, out_ref):
    moms, rows, width = half_ref.shape
    size = moms * rows
    nvec = width // 2
    per_step = out_ref.shape[0]
    left = half_ref[...].reshape(size, width)
    to = lax.broadcasted_iota(jnp.int32, (size, size), 0)
    frm = lax.broadcasted_iota(jnp.int32, (size, size), 1)
    swap = jnp.where((to // moms == frm % rows) & (to % moms == frm // rows), 1.0, 0.0).astype(jnp.bfloat16)
    left = jnp.dot(swap, left, preferred_element_type=jnp.float32)
    mreal = left[:, :nvec]
    mimag = left[:, nvec:]
    both = jnp.concatenate(
        [jnp.concatenate([mreal, -mimag], axis=1), jnp.concatenate([mimag, mreal], axis=1)], axis=0
    ).astype(jnp.bfloat16)
    for c in range(per_step):
        right = chosen_ref[c].reshape(width, nvec)
        prod = jnp.dot(both, right, preferred_element_type=jnp.float32)
        prod = jnp.where(pl.program_id(0) * per_step + c < counts_ref[0], prod, 0.0)
        out_ref[c, :, :, :nvec] = prod[:size].reshape(rows, moms, nvec)
        out_ref[c, :, :, nvec:] = prod[size:].reshape(rows, moms, nvec)


def per_device(evecs, peram, mom, pairs, counts):
    tcount, _, colours, piece_len, nvec = evecs.shape
    n_tm = lax.axis_size("tm")
    n_space = lax.axis_size("space")
    n_band = lax.axis_size("band")
    slots = pairs.shape[1]
    rows = nvec // n_space
    width = 2 * nvec
    base = ((lax.axis_index("tm") * n_space + lax.axis_index("space")) * piece_len).astype(jnp.int32)
    smem = pl.BlockSpec(memory_space=pltpu.SMEM)
    vmem = pl.BlockSpec(memory_space=pltpu.VMEM)
    hbm = pl.BlockSpec(memory_space=pl.ANY)
    parts, chosen = pl.pallas_call(
        gram_kernel,
        grid=(tcount,),
        in_specs=[
            smem,
            smem,
            smem,
            pl.BlockSpec((1, 2, colours, piece_len, nvec), lambda t: (t, 0, 0, 0, 0)),
            hbm,
        ],
        out_specs=[pl.BlockSpec((nvec, width), lambda t: (t, 0)), hbm],
        out_shape=[
            jax.ShapeDtypeStruct((tcount * nvec, width), jnp.bfloat16),
            jax.ShapeDtypeStruct((slots, 2, nvec, nvec), jnp.bfloat16),
        ],
        scratch_shapes=[
            pltpu.VMEM((piece_len, nvec), jnp.float32),
            pltpu.VMEM((piece_len, nvec), jnp.float32),
            pltpu.SemaphoreType.DMA((slots,)),
        ],
        compiler_params=pltpu.CompilerParams(vmem_limit_bytes=16 << 20),
        name="gram",
    )(base.reshape(1), mom, pairs, evecs, peram[0])
    parts = parts.reshape(n_tm * n_space, rows, width)
    parts = lax.all_to_all(parts, ("tm", "space"), 0, 0, tiled=True)
    meson, half = pl.pallas_call(
        sum_kernel,
        in_specs=[vmem],
        out_specs=[vmem, vmem],
        out_shape=[
            jax.ShapeDtypeStruct((rows, 1, width), jnp.float32),
            jax.ShapeDtypeStruct((n_band, rows, width), jnp.bfloat16),
        ],
        compiler_params=pltpu.CompilerParams(vmem_limit_bytes=8 << 20),
        name="total",
    )(parts)
    half = lax.all_to_all(half, "band", 0, 0, tiled=True)
    per_step = 2 if slots % 2 == 0 else 1
    blocks = pl.pallas_call(
        block_kernel,
        grid=(slots // per_step,),
        in_specs=[
            smem,
            vmem,
            pl.BlockSpec((per_step, 2, nvec, nvec), lambda c: (c, 0, 0, 0)),
        ],
        out_specs=pl.BlockSpec((per_step, rows, n_band, width), lambda c: (c, 0, 0, 0)),
        out_shape=jax.ShapeDtypeStruct((slots, rows, n_band, width), jnp.float32),
        compiler_params=pltpu.CompilerParams(vmem_limit_bytes=8 << 20),
        name="blocks",
    )(counts, half, chosen)
    return meson[None], blocks[None]


def solution(mesh):
    return jax.shard_map(
        per_device,
        mesh=mesh,
        in_specs=(
            P(None, None, None, ("tm", "space"), None),
            P("tm", None, None, None, None),
            P("band", None),
            P("band", None),
            P("band"),
        ),
        out_specs=(P("tm", "space", "band", None), P("tm", "band", "space", None, None)),
        check_vma=False,
    )
```

```python
import math

import jax
import jax.numpy as jnp
from jax import lax
from jax.experimental import pallas as pl
from jax.experimental.pallas import tpu as pltpu
from jax.sharding import PartitionSpec as P

EXTENT = 64


def gram_kernel(
    base_ref, mom_hbm, pairs_hbm, evecs_hbm, peram_hbm, out_ref, chosen_ref,
    evecs_ref, right_ref, mom_ref, pairs_ref, evecs_sems, small_sems, pick_sems,
):
    tcount, _, colours, sites, nvec = evecs_ref.shape
    slots = chosen_ref.shape[0]
    small = [
        pltpu.make_async_copy(mom_hbm, mom_ref, small_sems.at[0]),
        pltpu.make_async_copy(pairs_hbm, pairs_ref, small_sems.at[1]),
    ]
    loads = [
        pltpu.make_async_copy(evecs_hbm.at[t], evecs_ref.at[t], evecs_sems.at[t]) for t in range(tcount)
    ]
    for copy in small + loads:
        copy.start()
    site = base_ref[0] + lax.broadcasted_iota(jnp.int32, (sites, nvec), 0)
    xs = site & (EXTENT - 1)
    ys = (site >> 6) & (EXTENT - 1)
    zs = site >> 12
    for copy in small:
        copy.wait()
    picks = [
        pltpu.make_async_copy(peram_hbm.at[pairs_ref[0, c]], chosen_ref.at[c], pick_sems.at[c])
        for c in range(slots)
    ]
    for copy in picks:
        copy.start()
    wave = (mom_ref[0, 0] * xs + mom_ref[0, 1] * ys + mom_ref[0, 2] * zs) & (EXTENT - 1)
    theta = wave.astype(jnp.float32) * jnp.float32(2.0 * math.pi / EXTENT)
    cosine = jnp.cos(theta)
    sine = jnp.sin(theta)
    for t in range(tcount):
        loads[t].wait()
        slot = t % 2
        for colour in range(colours):
            vreal = evecs_ref[t, 0, colour].astype(jnp.float32)
            vimag = evecs_ref[t, 1, colour].astype(jnp.float32)
            wreal = (cosine * vreal + sine * vimag).astype(jnp.bfloat16)
            wimag = (cosine * vimag - sine * vreal).astype(jnp.bfloat16)
            right_ref[slot, 0, colour, :, :nvec] = wreal
            right_ref[slot, 0, colour, :, nvec:] = wimag
            right_ref[slot, 1, colour, :, :nvec] = wimag
            right_ref[slot, 1, colour, :, nvec:] = -wreal
        acc = lax.dot_general(
            evecs_ref[t].reshape(2 * colours * sites, nvec),
            right_ref[slot].reshape(2 * colours * sites, 2 * nvec),
            (((0,), (0,)), ((), ())),
            preferred_element_type=jnp.float32,
        )
        out_ref[t * nvec : (t + 1) * nvec] = acc.astype(out_ref.dtype)
    for copy in picks:
        copy.wait()


def sum_kernel(parts_ref, meson_ref, half_ref):
    total = jnp.sum(parts_ref[...].astype(jnp.float32), axis=0)
    half = total.astype(jnp.bfloat16)
    for row in range(total.shape[0]):
        meson_ref[row] = total[row : row + 1]
    for band in range(half_ref.shape[0]):
        half_ref[band] = half


def block_kernel(counts_ref, half_ref, chosen_ref, out_ref):
    moms, rows, width = half_ref.shape
    size = moms * rows
    nvec = width // 2
    per_step = out_ref.shape[0]
    left = half_ref[...].reshape(size, width)
    to = lax.broadcasted_iota(jnp.int32, (size, size), 0)
    frm = lax.broadcasted_iota(jnp.int32, (size, size), 1)
    swap = jnp.where((to // moms == frm % rows) & (to % moms == frm // rows), 1.0, 0.0).astype(jnp.bfloat16)
    left = jnp.dot(swap, left, preferred_element_type=jnp.float32)
    mreal = left[:, :nvec]
    mimag = left[:, nvec:]
    both = jnp.concatenate(
        [jnp.concatenate([mreal, -mimag], axis=1), jnp.concatenate([mimag, mreal], axis=1)], axis=0
    ).astype(jnp.bfloat16)
    for c in range(per_step):
        right = chosen_ref[c].reshape(width, nvec)
        prod = jnp.dot(both, right, preferred_element_type=jnp.float32)
        prod = jnp.where(pl.program_id(0) * per_step + c < counts_ref[0], prod, 0.0)
        out_ref[c, :, :, :nvec] = prod[:size].reshape(rows, moms, nvec)
        out_ref[c, :, :, nvec:] = prod[size:].reshape(rows, moms, nvec)


def per_device(evecs, peram, mom, pairs, counts):
    tcount, _, colours, piece_len, nvec = evecs.shape
    n_tm = lax.axis_size("tm")
    n_space = lax.axis_size("space")
    n_band = lax.axis_size("band")
    slots = pairs.shape[1]
    rows = nvec // n_space
    width = 2 * nvec
    base = ((lax.axis_index("tm") * n_space + lax.axis_index("space")) * piece_len).astype(jnp.int32)
    smem = pl.BlockSpec(memory_space=pltpu.SMEM)
    vmem = pl.BlockSpec(memory_space=pltpu.VMEM)
    hbm = pl.BlockSpec(memory_space=pltpu.HBM)
    parts, chosen = pl.pallas_call(
        gram_kernel,
        in_specs=[smem, hbm, hbm, hbm, hbm],
        out_specs=[vmem, vmem],
        out_shape=[
            jax.ShapeDtypeStruct((tcount * nvec, width), jnp.bfloat16),
            jax.ShapeDtypeStruct((slots, 2, nvec, nvec), jnp.bfloat16),
        ],
        scratch_shapes=[
            pltpu.VMEM((tcount, 2, colours, piece_len, nvec), jnp.bfloat16),
            pltpu.VMEM((2, 2, colours, piece_len, width), jnp.bfloat16),
            pltpu.SMEM(mom.shape, jnp.int32),
            pltpu.SMEM(pairs.shape, jnp.int32),
            pltpu.SemaphoreType.DMA((tcount,)),
            pltpu.SemaphoreType.DMA((2,)),
            pltpu.SemaphoreType.DMA((slots,)),
        ],
        compiler_params=pltpu.CompilerParams(vmem_limit_bytes=16 << 20),
        name="gram",
    )(base.reshape(1), *(pltpu.with_memory_space_constraint(a, pltpu.HBM) for a in (mom, pairs, evecs, peram[0])))
    parts = parts.reshape(n_tm * n_space, rows, width)
    parts = lax.all_to_all(parts, ("tm", "space"), 0, 0, tiled=True)
    meson, half = pl.pallas_call(
        sum_kernel,
        in_specs=[vmem],
        out_specs=[vmem, vmem],
        out_shape=[
            jax.ShapeDtypeStruct((rows, 1, width), jnp.float32),
            jax.ShapeDtypeStruct((n_band, rows, width), jnp.bfloat16),
        ],
        compiler_params=pltpu.CompilerParams(vmem_limit_bytes=8 << 20),
        name="total",
    )(parts)
    half = lax.all_to_all(half, "band", 0, 0, tiled=True)
    per_step = 2 if slots % 2 == 0 else 1
    blocks = pl.pallas_call(
        block_kernel,
        grid=(slots // per_step,),
        in_specs=[
            smem,
            vmem,
            pl.BlockSpec((per_step, 2, nvec, nvec), lambda c: (c, 0, 0, 0)),
        ],
        out_specs=pl.BlockSpec((per_step, rows, n_band, width), lambda c: (c, 0, 0, 0)),
        out_shape=jax.ShapeDtypeStruct((slots, rows, n_band, width), jnp.float32),
        compiler_params=pltpu.CompilerParams(vmem_limit_bytes=8 << 20),
        name="blocks",
    )(counts, half, chosen)
    return meson[None], blocks[None]


def solution(mesh):
    return jax.shard_map(
        per_device,
        mesh=mesh,
        in_specs=(
            P(None, None, None, ("tm", "space"), None),
            P("tm", None, None, None, None),
            P("band", None),
            P("band", None),
            P("band"),
        ),
        out_specs=(P("tm", "space", "band", None), P("tm", "band", "space", None, None)),
        check_vma=False,
    )
```

```python
import math

import jax
import jax.numpy as jnp
from jax import lax
from jax.experimental import pallas as pl
from jax.experimental.pallas import tpu as pltpu
from jax.sharding import Mesh, PartitionSpec as P

EXTENT = 64
Z_LO = 4


def gram_kernel(
    base_ref, mom_hbm, pairs_hbm, evecs_hbm, peram_hbm, out_ref, chosen_ref,
    evecs_ref, right_ref, mom_ref, pairs_ref, evecs_sems, small_sems, pick_sems,
):
    tcount, _, colours, sites, nvec = evecs_ref.shape
    slots = chosen_ref.shape[0]
    n_x = out_ref.shape[0] // tcount
    n_zl, rows = out_ref.shape[1:3]
    small = [
        pltpu.make_async_copy(mom_hbm, mom_ref, small_sems.at[0]),
        pltpu.make_async_copy(pairs_hbm, pairs_ref, small_sems.at[1]),
    ]
    loads = [
        pltpu.make_async_copy(evecs_hbm.at[t], evecs_ref.at[t], evecs_sems.at[t]) for t in range(tcount)
    ]
    for copy in small + loads:
        copy.start()
    site = base_ref[0] + lax.broadcasted_iota(jnp.int32, (sites, nvec), 0)
    xs = site & (EXTENT - 1)
    ys = (site >> 6) & (EXTENT - 1)
    zs = site >> 12
    for copy in small:
        copy.wait()
    picks = [
        pltpu.make_async_copy(peram_hbm.at[pairs_ref[0, c]], chosen_ref.at[c], pick_sems.at[c])
        for c in range(slots)
    ]
    for copy in picks:
        copy.start()
    wave = (mom_ref[0, 0] * xs + mom_ref[0, 1] * ys + mom_ref[0, 2] * zs) & (EXTENT - 1)
    theta = wave.astype(jnp.float32) * jnp.float32(2.0 * math.pi / EXTENT)
    cosine = jnp.cos(theta)
    sine = jnp.sin(theta)
    for t in range(tcount):
        loads[t].wait()
        slot = t % 2
        for colour in range(colours):
            real = evecs_ref[t, 0, colour]
            imag = evecs_ref[t, 1, colour]
            vreal = real.astype(jnp.float32)
            vimag = imag.astype(jnp.float32)
            right_ref[slot, colour, :, :nvec] = (cosine * vreal + sine * vimag).astype(jnp.bfloat16)
            right_ref[slot, colour, :, nvec:] = (cosine * vimag - sine * vreal).astype(jnp.bfloat16)
        acc = jnp.concatenate([lax.dot_general(
            evecs_ref[t, q].reshape(colours * sites, nvec),
            right_ref[slot].reshape(colours * sites, 2 * nvec),
            (((0,), (0,)), ((), ())),
            preferred_element_type=jnp.float32,
        ) for q in range(2)], axis=0)
        meson = jnp.concatenate(
            [acc[:nvec, :nvec] + acc[nvec:, nvec:], acc[:nvec, nvec:] - acc[nvec:, :nvec]], axis=1
        )
        meson = meson.astype(out_ref.dtype)
        for x in range(n_x):
            for zl in range(n_zl):
                first = (zl * n_x + x) * rows
                out_ref[t * n_x + x, zl] = meson[first : first + rows]
    for copy in picks:
        copy.wait()


def sum_kernel(parts_ref, out_ref):
    total = jnp.sum(parts_ref[...].astype(jnp.float32), axis=0).astype(jnp.bfloat16)
    for band in range(out_ref.shape[0]):
        out_ref[band] = total


def block_kernel(band_ref, counts_ref, parts_ref, chosen_ref, meson_ref, out_hbm, total_ref, out_ref, sems):
    moms, _, rows, width = parts_ref.shape
    slots = out_ref.shape[0]
    size = moms * rows
    nvec = width // 2
    total_ref[...] = jnp.sum(parts_ref[...].astype(jnp.float32), axis=1)
    left = total_ref[...].astype(jnp.bfloat16).reshape(size, width)
    to = lax.broadcasted_iota(jnp.int32, (size, size), 0)
    frm = lax.broadcasted_iota(jnp.int32, (size, size), 1)
    swap = jnp.where((to // moms == frm % rows) & (to % moms == frm // rows), 1.0, 0.0).astype(jnp.bfloat16)
    left = jnp.dot(swap, left, preferred_element_type=jnp.float32)
    mreal = left[:, :nvec]
    mimag = left[:, nvec:]
    both = jnp.concatenate(
        [jnp.concatenate([mreal, -mimag], axis=1), jnp.concatenate([mimag, mreal], axis=1)], axis=0
    ).astype(jnp.bfloat16)
    copies = []
    for c in range(slots):
        right = chosen_ref[c].reshape(width, nvec)
        prod = jnp.dot(both, right, preferred_element_type=jnp.float32)
        prod = jnp.where(c < counts_ref[0], prod, 0.0)
        out_ref[c, :, :, :nvec] = prod[:size].reshape(rows, moms, nvec)
        out_ref[c, :, :, nvec:] = prod[size:].reshape(rows, moms, nvec)
        copies.append(pltpu.make_async_copy(out_ref.at[c], out_hbm.at[c], sems.at[c]))
        copies[-1].start()
    own = total_ref[band_ref[0]]
    for row in range(rows):
        meson_ref[row] = own[row : row + 1]
    for copy in copies:
        copy.wait()


def per_device(evecs, peram, mom, pairs, counts):
    tcount, _, colours, piece_len, nvec = evecs.shape
    n_tm = lax.axis_size("tm")
    n_zl = lax.axis_size("z_lo")
    n_x = lax.axis_size("x")
    n_band = lax.axis_size("band")
    slots = pairs.shape[1]
    rows = nvec // (n_zl * n_x)
    width = 2 * nvec
    place = (lax.axis_index("tm") * n_zl + lax.axis_index("z_lo")) * n_x + lax.axis_index("x")
    base = (place * piece_len).astype(jnp.int32)
    smem = pl.BlockSpec(memory_space=pltpu.SMEM)
    vmem = pl.BlockSpec(memory_space=pltpu.VMEM)
    hbm = pl.BlockSpec(memory_space=pltpu.HBM)
    parts, chosen = pl.pallas_call(
        gram_kernel,
        in_specs=[smem, hbm, hbm, hbm, hbm],
        out_specs=[vmem, vmem],
        out_shape=[
            jax.ShapeDtypeStruct((n_tm * n_x, n_zl, rows, width), jnp.bfloat16),
            jax.ShapeDtypeStruct((slots, 2, nvec, nvec), jnp.bfloat16),
        ],
        scratch_shapes=[
            pltpu.VMEM((tcount, 2, colours, piece_len, nvec), jnp.bfloat16),
            pltpu.VMEM((2, colours, piece_len, width), jnp.bfloat16),
            pltpu.SMEM(mom.shape, jnp.int32),
            pltpu.SMEM(pairs.shape, jnp.int32),
            pltpu.SemaphoreType.DMA((tcount,)),
            pltpu.SemaphoreType.DMA((2,)),
            pltpu.SemaphoreType.DMA((slots,)),
        ],
        compiler_params=pltpu.CompilerParams(vmem_limit_bytes=16 << 20),
        name="gram",
    )(base.reshape(1), *(pltpu.with_memory_space_constraint(a, pltpu.HBM) for a in (mom, pairs, evecs, peram[0])))
    parts = lax.all_to_all(parts, ("tm", "x"), 0, 0, tiled=True)
    parts = pl.pallas_call(
        sum_kernel,
        in_specs=[vmem],
        out_specs=vmem,
        out_shape=jax.ShapeDtypeStruct((n_band, n_zl, rows, width), jnp.bfloat16),
        compiler_params=pltpu.CompilerParams(vmem_limit_bytes=8 << 20),
        name="total",
    )(parts)
    parts = parts.reshape(n_band * n_zl, rows, width)
    parts = lax.all_to_all(parts, ("band", "z_lo"), 0, 0, tiled=True)
    meson, blocks = pl.pallas_call(
        block_kernel,
        in_specs=[smem, smem, vmem, vmem],
        out_specs=[vmem, hbm],
        out_shape=[
            jax.ShapeDtypeStruct((rows, 1, width), jnp.float32),
            jax.ShapeDtypeStruct((slots, rows, n_band, width), jnp.float32),
        ],
        scratch_shapes=[
            pltpu.VMEM((n_band, rows, width), jnp.float32),
            pltpu.VMEM((slots, rows, n_band, width), jnp.float32),
            pltpu.SemaphoreType.DMA((slots,)),
        ],
        compiler_params=pltpu.CompilerParams(vmem_limit_bytes=8 << 20),
        name="blocks",
    )(
        lax.axis_index("band").astype(jnp.int32).reshape(1),
        counts,
        parts.reshape(n_band, n_zl, rows, width),
        chosen,
    )
    return meson[None], blocks[None]


def solution(mesh):
    n_tm, n_band, n_space = (mesh.shape[name] for name in ("tm", "band", "space"))
    fine = Mesh(mesh.devices.reshape(n_tm, n_band, Z_LO, n_space // Z_LO), ("tm", "band", "z_lo", "x"))
    return jax.shard_map(
        per_device,
        mesh=fine,
        in_specs=(
            P(None, None, None, ("tm", "z_lo", "x"), None),
            P("tm", None, None, None, None),
            P("band", None),
            P("band", None),
            P("band"),
        ),
        out_specs=(P("tm", ("z_lo", "x"), "band", None), P("tm", "band", ("z_lo", "x"), None, None)),
        check_vma=False,
    )
```

```python
import math

import jax
import jax.numpy as jnp
from jax import lax
from jax.experimental import pallas as pl
from jax.experimental.pallas import tpu as pltpu
from jax.sharding import Mesh, PartitionSpec as P

EXTENT = 64
Z_LO = 4


def gram_kernel(
    base_ref, mom_hbm, pairs_hbm, evecs_hbm, peram_hbm, out_ref, chosen_ref,
    evecs_ref, right_ref, mom_ref, pairs_ref, evecs_sems, small_sems, pick_sems,
):
    tcount, _, colours, sites, nvec = evecs_ref.shape
    slots = chosen_ref.shape[0]
    n_x = out_ref.shape[0] // tcount
    n_zl, rows = out_ref.shape[1:3]
    small = [
        pltpu.make_async_copy(mom_hbm, mom_ref, small_sems.at[0]),
        pltpu.make_async_copy(pairs_hbm, pairs_ref, small_sems.at[1]),
    ]
    loads = [
        pltpu.make_async_copy(evecs_hbm.at[t], evecs_ref.at[t], evecs_sems.at[t]) for t in range(tcount)
    ]
    for copy in small + loads:
        copy.start()
    site = base_ref[0] + lax.broadcasted_iota(jnp.int32, (sites, nvec), 0)
    xs = site & (EXTENT - 1)
    ys = (site >> 6) & (EXTENT - 1)
    zs = site >> 12
    for copy in small:
        copy.wait()
    picks = [
        pltpu.make_async_copy(peram_hbm.at[pairs_ref[0, c]], chosen_ref.at[c], pick_sems.at[c])
        for c in range(slots)
    ]
    for copy in picks:
        copy.start()
    wave = (mom_ref[0, 0] * xs + mom_ref[0, 1] * ys + mom_ref[0, 2] * zs) & (EXTENT - 1)
    theta = wave.astype(jnp.float32) * jnp.float32(2.0 * math.pi / EXTENT)
    cosine = jnp.cos(theta)
    sine = jnp.sin(theta)

    def rotate(t):
        for colour in range(colours):
            vreal = evecs_ref[t, 0, colour].astype(jnp.float32)
            vimag = evecs_ref[t, 1, colour].astype(jnp.float32)
            right_ref[t, colour, :, :nvec] = (cosine * vreal + sine * vimag).astype(jnp.bfloat16)
            right_ref[t, colour, :, nvec:] = (cosine * vimag - sine * vreal).astype(jnp.bfloat16)

    def multiply(t):
        right = right_ref[t].reshape(colours * sites, 2 * nvec)
        with_real, with_imag = (
            lax.dot_general(
                evecs_ref[t, part].reshape(colours * sites, nvec),
                right,
                (((0,), (0,)), ((), ())),
                preferred_element_type=jnp.float32,
            )
            for part in range(2)
        )
        meson = jnp.concatenate(
            [with_real[:, :nvec] + with_imag[:, nvec:], with_real[:, nvec:] - with_imag[:, :nvec]], axis=1
        ).astype(out_ref.dtype)
        for x in range(n_x):
            for zl in range(n_zl):
                first = (zl * n_x + x) * rows
                out_ref[t * n_x + x, zl] = meson[first : first + rows]

    groups = [list(range(4)), list(range(4, 8))]
    for g, group in enumerate(groups):
        for t in group:
            loads[t].wait()
        for t in group:
            rotate(t)
            multiply(t)
    for copy in picks:
        copy.wait()


def sum_kernel(parts_ref, out_ref):
    total = jnp.sum(parts_ref[...].astype(jnp.float32), axis=0).astype(jnp.bfloat16)
    for band in range(out_ref.shape[0]):
        out_ref[band] = total


def block_kernel(band_ref, counts_ref, parts_ref, chosen_ref, meson_hbm, out_hbm, total_ref, meson_ref, out_ref, sems):
    moms, _, rows, width = parts_ref.shape
    slots = out_ref.shape[0]
    size = moms * rows
    nvec = width // 2
    total_ref[...] = jnp.sum(parts_ref[...].astype(jnp.float32), axis=1)
    own = total_ref[band_ref[0]]
    for row in range(rows):
        meson_ref[row] = own[row : row + 1]
    meson_copy = pltpu.make_async_copy(meson_ref, meson_hbm, sems.at[slots])
    meson_copy.start()
    left = jnp.swapaxes(total_ref[...], 0, 1).reshape(size, width)
    mreal = left[:, :nvec]
    mimag = left[:, nvec:]
    both = jnp.concatenate(
        [jnp.concatenate([mreal, -mimag], axis=1), jnp.concatenate([mimag, mreal], axis=1)], axis=0
    ).astype(jnp.bfloat16)
    copies = [meson_copy]
    for pair in range(slots // 2):
        right = jnp.concatenate([chosen_ref[2 * pair + q].reshape(width, nvec) for q in range(2)], axis=1)
        prods = jnp.dot(both, right, preferred_element_type=jnp.float32)
        for q in range(2):
            c = 2 * pair + q
            prod = jnp.where(c < counts_ref[0], prods[:, q * nvec : (q + 1) * nvec], 0.0)
            out_ref[c, :, :, :nvec] = prod[:size].reshape(rows, moms, nvec)
            out_ref[c, :, :, nvec:] = prod[size:].reshape(rows, moms, nvec)
            copies.append(pltpu.make_async_copy(out_ref.at[c], out_hbm.at[c], sems.at[c]))
            copies[-1].start()
    for copy in copies:
        copy.wait()


def per_device(evecs, peram, mom, pairs, counts):
    tcount, _, colours, piece_len, nvec = evecs.shape
    n_tm = lax.axis_size("tm")
    n_zl = lax.axis_size("z_lo")
    n_x = lax.axis_size("x")
    n_band = lax.axis_size("band")
    slots = pairs.shape[1]
    rows = nvec // (n_zl * n_x)
    width = 2 * nvec
    place = (lax.axis_index("tm") * n_zl + lax.axis_index("z_lo")) * n_x + lax.axis_index("x")
    base = (place * piece_len).astype(jnp.int32)
    smem = pl.BlockSpec(memory_space=pltpu.SMEM)
    vmem = pl.BlockSpec(memory_space=pltpu.VMEM)
    hbm = pl.BlockSpec(memory_space=pltpu.HBM)
    parts, chosen = pl.pallas_call(
        gram_kernel,
        in_specs=[smem, hbm, hbm, hbm, hbm],
        out_specs=[vmem, vmem],
        out_shape=[
            jax.ShapeDtypeStruct((n_tm * n_x, n_zl, rows, width), jnp.bfloat16),
            jax.ShapeDtypeStruct((slots, 2, nvec, nvec), jnp.bfloat16),
        ],
        scratch_shapes=[
            pltpu.VMEM((tcount, 2, colours, piece_len, nvec), jnp.bfloat16),
            pltpu.VMEM((tcount, colours, piece_len, width), jnp.bfloat16),
            pltpu.SMEM(mom.shape, jnp.int32),
            pltpu.SMEM(pairs.shape, jnp.int32),
            pltpu.SemaphoreType.DMA((tcount,)),
            pltpu.SemaphoreType.DMA((2,)),
            pltpu.SemaphoreType.DMA((slots,)),
        ],
        compiler_params=pltpu.CompilerParams(vmem_limit_bytes=16 << 20),
        name="gram",
    )(base.reshape(1), *(pltpu.with_memory_space_constraint(a, pltpu.HBM) for a in (mom, pairs, evecs, peram[0])))
    parts = lax.all_to_all(parts, ("tm", "x"), 0, 0, tiled=True)
    parts = pl.pallas_call(
        sum_kernel,
        in_specs=[vmem],
        out_specs=vmem,
        out_shape=jax.ShapeDtypeStruct((n_band, n_zl, rows, width), jnp.bfloat16),
        compiler_params=pltpu.CompilerParams(vmem_limit_bytes=8 << 20),
        name="total",
    )(parts)
    parts = parts.reshape(n_band * n_zl, rows, width)
    parts = lax.all_to_all(parts, ("band", "z_lo"), 0, 0, tiled=True)
    meson, blocks = pl.pallas_call(
        block_kernel,
        in_specs=[smem, smem, vmem, vmem],
        out_specs=[hbm, hbm],
        out_shape=[
            jax.ShapeDtypeStruct((rows, 1, width), jnp.float32),
            jax.ShapeDtypeStruct((slots, rows, n_band, width), jnp.float32),
        ],
        scratch_shapes=[
            pltpu.VMEM((n_band, rows, width), jnp.float32),
            pltpu.VMEM((rows, 1, width), jnp.float32),
            pltpu.VMEM((slots, rows, n_band, width), jnp.float32),
            pltpu.SemaphoreType.DMA((slots + 1,)),
        ],
        compiler_params=pltpu.CompilerParams(vmem_limit_bytes=8 << 20),
        name="blocks",
    )(
        lax.axis_index("band").astype(jnp.int32).reshape(1),
        counts,
        parts.reshape(n_band, n_zl, rows, width),
        chosen,
    )
    return meson[None], blocks[None]


def solution(mesh):
    n_tm, n_band, n_space = (mesh.shape[name] for name in ("tm", "band", "space"))
    fine = Mesh(mesh.devices.reshape(n_tm, n_band, Z_LO, n_space // Z_LO), ("tm", "band", "z_lo", "x"))
    return jax.shard_map(
        per_device,
        mesh=fine,
        in_specs=(
            P(None, None, None, ("tm", "z_lo", "x"), None),
            P("tm", None, None, None, None),
            P("band", None),
            P("band", None),
            P("band"),
        ),
        out_specs=(P("tm", ("z_lo", "x"), "band", None), P("tm", "band", ("z_lo", "x"), None, None)),
        check_vma=False,
    )
```

```python
import math

import jax
import jax.numpy as jnp
from jax import lax
from jax.experimental import pallas as pl
from jax.experimental.pallas import tpu as pltpu
from jax.sharding import Mesh, PartitionSpec as P

EXTENT = 64
Z_LO = 4
CORES = 2


def gram_kernel(
    base_ref, mom_hbm, pairs_hbm, evecs_hbm, peram_hbm, out_ref, chosen_ref,
    evecs_ref, right_ref, mom_ref, pairs_ref, evecs_sems, small_sems, pick_sems,
):
    tcount, _, colours, sites, nvec = evecs_ref.shape
    slots = chosen_ref.shape[0]
    n_x = out_ref.shape[0] // tcount
    n_zl, rows = out_ref.shape[1:3]
    small = [
        pltpu.make_async_copy(mom_hbm, mom_ref, small_sems.at[0]),
        pltpu.make_async_copy(pairs_hbm, pairs_ref, small_sems.at[1]),
    ]
    loads = [
        pltpu.make_async_copy(evecs_hbm.at[t], evecs_ref.at[t], evecs_sems.at[t]) for t in range(tcount)
    ]
    for copy in small + loads:
        copy.start()
    site = base_ref[0] + lax.broadcasted_iota(jnp.int32, (sites, nvec), 0)
    xs = site & (EXTENT - 1)
    ys = (site >> 6) & (EXTENT - 1)
    zs = site >> 12
    for copy in small:
        copy.wait()
    picks = [
        pltpu.make_async_copy(peram_hbm.at[pairs_ref[0, c]], chosen_ref.at[c], pick_sems.at[c])
        for c in range(slots)
    ]
    for copy in picks:
        copy.start()
    wave = (mom_ref[0, 0] * xs + mom_ref[0, 1] * ys + mom_ref[0, 2] * zs) & (EXTENT - 1)
    theta = wave.astype(jnp.float32) * jnp.float32(2.0 * math.pi / EXTENT)
    cosine = jnp.cos(theta)
    sine = jnp.sin(theta)

    def rotate(t):
        for colour in range(colours):
            vreal = evecs_ref[t, 0, colour].astype(jnp.float32)
            vimag = evecs_ref[t, 1, colour].astype(jnp.float32)
            right_ref[t, colour, :, :nvec] = (cosine * vreal + sine * vimag).astype(jnp.bfloat16)
            right_ref[t, colour, :, nvec:] = (cosine * vimag - sine * vreal).astype(jnp.bfloat16)

    def multiply(t):
        right = right_ref[t].reshape(colours * sites, 2 * nvec)
        with_real, with_imag = (
            lax.dot_general(
                evecs_ref[t, part].reshape(colours * sites, nvec),
                right,
                (((0,), (0,)), ((), ())),
                preferred_element_type=jnp.float32,
            )
            for part in range(2)
        )
        meson = jnp.concatenate(
            [with_real[:, :nvec] + with_imag[:, nvec:], with_real[:, nvec:] - with_imag[:, :nvec]], axis=1
        ).astype(out_ref.dtype)
        for x in range(n_x):
            for zl in range(n_zl):
                first = (zl * n_x + x) * rows
                out_ref[x * tcount + t, zl] = meson[first : first + rows]

    groups = [list(range(4)), list(range(4, 8))]
    for g, group in enumerate(groups):
        for t in group:
            loads[t].wait()
        for t in group:
            rotate(t)
            multiply(t)
    for copy in picks:
        copy.wait()


def sum_kernel(parts_ref, out_ref):
    total = jnp.sum(parts_ref[...].astype(jnp.float32), axis=0).astype(jnp.bfloat16)
    for band in range(out_ref.shape[0]):
        out_ref[band] = total


def block_kernel(band_ref, counts_ref, parts_ref, chosen_ref, meson_hbm, out_hbm, total_ref, meson_ref, out_ref, sems):
    cores, n_zh, _, rows, width = parts_ref.shape
    moms = cores * n_zh
    slots = out_ref.shape[0]
    size = moms * rows
    nvec = width // 2
    for core in range(cores):
        for zh in range(n_zh):
            total_ref[zh * cores + core] = jnp.sum(parts_ref[core, zh].astype(jnp.float32), axis=0)
    own = total_ref[band_ref[0]]
    for row in range(rows):
        meson_ref[row] = own[row : row + 1]
    meson_copy = pltpu.make_async_copy(meson_ref, meson_hbm, sems.at[slots])
    meson_copy.start()
    left = jnp.swapaxes(total_ref[...], 0, 1).reshape(size, width)
    mreal = left[:, :nvec]
    mimag = left[:, nvec:]
    both = jnp.concatenate(
        [jnp.concatenate([mreal, -mimag], axis=1), jnp.concatenate([mimag, mreal], axis=1)], axis=0
    ).astype(jnp.bfloat16)
    copies = [meson_copy]
    for pair in range(slots // 2):
        right = jnp.concatenate([chosen_ref[2 * pair + q].reshape(width, nvec) for q in range(2)], axis=1)
        prods = jnp.dot(both, right, preferred_element_type=jnp.float32)
        for q in range(2):
            c = 2 * pair + q
            prod = jnp.where(c < counts_ref[0], prods[:, q * nvec : (q + 1) * nvec], 0.0)
            out_ref[c, :, :, :nvec] = prod[:size].reshape(rows, moms, nvec)
            out_ref[c, :, :, nvec:] = prod[size:].reshape(rows, moms, nvec)
            copies.append(pltpu.make_async_copy(out_ref.at[c], out_hbm.at[c], sems.at[c]))
            copies[-1].start()
    for copy in copies:
        copy.wait()


def per_device(evecs, peram, mom, pairs, counts):
    tcount, _, colours, piece_len, nvec = evecs.shape
    n_tm = lax.axis_size("tm")
    n_zl = lax.axis_size("z_lo")
    n_x = lax.axis_size("x")
    n_zh = lax.axis_size("z_hi")
    n_core = lax.axis_size("core")
    n_band = n_zh * n_core
    slots = pairs.shape[1]
    rows = nvec // (n_zl * n_x)
    width = 2 * nvec
    place = (lax.axis_index("tm") * n_zl + lax.axis_index("z_lo")) * n_x + lax.axis_index("x")
    base = (place * piece_len).astype(jnp.int32)
    smem = pl.BlockSpec(memory_space=pltpu.SMEM)
    vmem = pl.BlockSpec(memory_space=pltpu.VMEM)
    hbm = pl.BlockSpec(memory_space=pltpu.HBM)
    parts, chosen = pl.pallas_call(
        gram_kernel,
        in_specs=[smem, hbm, hbm, hbm, hbm],
        out_specs=[vmem, vmem],
        out_shape=[
            jax.ShapeDtypeStruct((n_tm * n_x, n_zl, rows, width), jnp.bfloat16),
            jax.ShapeDtypeStruct((slots, 2, nvec, nvec), jnp.bfloat16),
        ],
        scratch_shapes=[
            pltpu.VMEM((tcount, 2, colours, piece_len, nvec), jnp.bfloat16),
            pltpu.VMEM((tcount, colours, piece_len, width), jnp.bfloat16),
            pltpu.SMEM(mom.shape, jnp.int32),
            pltpu.SMEM(pairs.shape, jnp.int32),
            pltpu.SemaphoreType.DMA((tcount,)),
            pltpu.SemaphoreType.DMA((2,)),
            pltpu.SemaphoreType.DMA((slots,)),
        ],
        compiler_params=pltpu.CompilerParams(vmem_limit_bytes=16 << 20),
        name="gram",
    )(base.reshape(1), *(pltpu.with_memory_space_constraint(a, pltpu.HBM) for a in (mom, pairs, evecs, peram[0])))
    parts = lax.all_to_all(parts, ("x", "tm"), 0, 0, tiled=True)
    parts = pl.pallas_call(
        sum_kernel,
        in_specs=[vmem],
        out_specs=vmem,
        out_shape=jax.ShapeDtypeStruct((n_band, n_zl, rows, width), jnp.bfloat16),
        compiler_params=pltpu.CompilerParams(vmem_limit_bytes=8 << 20),
        name="total",
    )(parts)
    parts = parts.reshape(n_band * n_zl, rows, width)
    parts = lax.all_to_all(parts, ("core", "z_hi", "z_lo"), 0, 0, tiled=True)
    meson, blocks = pl.pallas_call(
        block_kernel,
        in_specs=[smem, smem, vmem, vmem],
        out_specs=[hbm, hbm],
        out_shape=[
            jax.ShapeDtypeStruct((rows, 1, width), jnp.float32),
            jax.ShapeDtypeStruct((slots, rows, n_band, width), jnp.float32),
        ],
        scratch_shapes=[
            pltpu.VMEM((n_band, rows, width), jnp.float32),
            pltpu.VMEM((rows, 1, width), jnp.float32),
            pltpu.VMEM((slots, rows, n_band, width), jnp.float32),
            pltpu.SemaphoreType.DMA((slots + 1,)),
        ],
        compiler_params=pltpu.CompilerParams(vmem_limit_bytes=8 << 20),
        name="blocks",
    )(
        (lax.axis_index("z_hi") * n_core + lax.axis_index("core")).astype(jnp.int32).reshape(1),
        counts,
        parts.reshape(n_core, n_zh, n_zl, rows, width),
        chosen,
    )
    return meson[None], blocks[None]


def solution(mesh):
    n_tm, n_band, n_space = (mesh.shape[name] for name in ("tm", "band", "space"))
    fine = Mesh(
        mesh.devices.reshape(n_tm, n_band // CORES, CORES, Z_LO, n_space // Z_LO),
        ("tm", "z_hi", "core", "z_lo", "x"),
    )
    band = ("z_hi", "core")
    return jax.shard_map(
        per_device,
        mesh=fine,
        in_specs=(
            P(None, None, None, ("tm", "z_lo", "x"), None),
            P("tm", None, None, None, None),
            P(band, None),
            P(band, None),
            P(band),
        ),
        out_specs=(P("tm", ("z_lo", "x"), band, None), P("tm", band, ("z_lo", "x"), None, None)),
        check_vma=False,
    )
```

```python
import math

import jax
import jax.numpy as jnp
from jax import lax
from jax.experimental import pallas as pl
from jax.experimental.pallas import tpu as pltpu
from jax.sharding import Mesh, PartitionSpec as P

EXTENT = 64
Z_LO = 4
CORES = 2


def gram_kernel(
    base_ref, mom_hbm, pairs_hbm, evecs_hbm, peram_hbm, out_ref, chosen_ref,
    evecs_ref, right_ref, mom_ref, pairs_ref, evecs_sems, small_sems, pick_sems,
):
    tcount, _, colours, sites, nvec = evecs_ref.shape
    slots = chosen_ref.shape[0]
    n_x = out_ref.shape[0] // tcount
    n_zl, rows = out_ref.shape[1:3]
    small = [
        pltpu.make_async_copy(mom_hbm, mom_ref, small_sems.at[0]),
        pltpu.make_async_copy(pairs_hbm, pairs_ref, small_sems.at[1]),
    ]
    loads = [
        pltpu.make_async_copy(evecs_hbm.at[t], evecs_ref.at[t], evecs_sems.at[t]) for t in range(tcount)
    ]
    for copy in small + loads:
        copy.start()
    site = base_ref[0] + lax.broadcasted_iota(jnp.int32, (sites, nvec), 0)
    xs = site & (EXTENT - 1)
    ys = (site >> 6) & (EXTENT - 1)
    zs = site >> 12
    for copy in small:
        copy.wait()
    picks = [
        pltpu.make_async_copy(peram_hbm.at[pairs_ref[0, c]], chosen_ref.at[c], pick_sems.at[c])
        for c in range(slots)
    ]
    for copy in picks:
        copy.start()
    wave = (mom_ref[0, 0] * xs + mom_ref[0, 1] * ys + mom_ref[0, 2] * zs) & (EXTENT - 1)
    theta = wave.astype(jnp.float32) * jnp.float32(2.0 * math.pi / EXTENT)
    cosine = jnp.cos(theta)
    sine = jnp.sin(theta)

    def rotate(t):
        for colour in range(colours):
            vreal = evecs_ref[t, 0, colour].astype(jnp.float32)
            vimag = evecs_ref[t, 1, colour].astype(jnp.float32)
            right_ref[t, colour, :, :nvec] = (cosine * vreal + sine * vimag).astype(jnp.bfloat16)
            right_ref[t, colour, :, nvec:] = (cosine * vimag - sine * vreal).astype(jnp.bfloat16)

    def multiply(t):
        right = right_ref[t].reshape(colours * sites, 2 * nvec)
        with_real, with_imag = (
            lax.dot_general(
                evecs_ref[t, part].reshape(colours * sites, nvec),
                right,
                (((0,), (0,)), ((), ())),
                preferred_element_type=jnp.float32,
            )
            for part in range(2)
        )
        meson = jnp.concatenate(
            [with_real[:, :nvec] + with_imag[:, nvec:], with_real[:, nvec:] - with_imag[:, :nvec]], axis=1
        ).astype(out_ref.dtype)
        for x in range(n_x):
            for zl in range(n_zl):
                first = (zl * n_x + x) * rows
                out_ref[x * tcount + t, zl] = meson[first : first + rows]

    groups = [list(range(4)), list(range(4, 8))]
    for g, group in enumerate(groups):
        for t in group:
            loads[t].wait()
        for t in group:
            rotate(t)
            multiply(t)
    for copy in picks:
        copy.wait()


def sum_kernel(parts_ref, out_ref):
    total = jnp.sum(parts_ref[...].astype(jnp.float32), axis=0).astype(jnp.bfloat16)
    for zh in range(out_ref.shape[0]):
        for core in range(out_ref.shape[2]):
            out_ref[zh, :, core] = total


def block_kernel(band_ref, counts_ref, parts_ref, chosen_ref, meson_hbm, out_hbm, total_ref, meson_ref, out_ref, sems):
    n_zh, _, cores, rows, width = parts_ref.shape
    moms = cores * n_zh
    slots = out_ref.shape[0]
    size = moms * rows
    nvec = width // 2
    for core in range(cores):
        for zh in range(n_zh):
            total_ref[zh * cores + core] = jnp.sum(parts_ref[zh, :, core].astype(jnp.float32), axis=0)
    own = total_ref[band_ref[0]]
    for row in range(rows):
        meson_ref[row] = own[row : row + 1]
    meson_copy = pltpu.make_async_copy(meson_ref, meson_hbm, sems.at[slots])
    meson_copy.start()
    left = jnp.swapaxes(total_ref[...], 0, 1).reshape(size, width)
    mreal = left[:, :nvec]
    mimag = left[:, nvec:]
    both = jnp.concatenate(
        [jnp.concatenate([mreal, -mimag], axis=1), jnp.concatenate([mimag, mreal], axis=1)], axis=0
    ).astype(jnp.bfloat16)
    copies = [meson_copy]
    for pair in range(slots // 2):
        right = jnp.concatenate([chosen_ref[2 * pair + q].reshape(width, nvec) for q in range(2)], axis=1)
        prods = jnp.dot(both, right, preferred_element_type=jnp.float32)
        for q in range(2):
            c = 2 * pair + q
            prod = jnp.where(c < counts_ref[0], prods[:, q * nvec : (q + 1) * nvec], 0.0)
            out_ref[c, :, :, :nvec] = prod[:size].reshape(rows, moms, nvec)
            out_ref[c, :, :, nvec:] = prod[size:].reshape(rows, moms, nvec)
            copies.append(pltpu.make_async_copy(out_ref.at[c], out_hbm.at[c], sems.at[c]))
            copies[-1].start()
    for copy in copies:
        copy.wait()


def per_device(evecs, peram, mom, pairs, counts):
    tcount, _, colours, piece_len, nvec = evecs.shape
    n_tm = lax.axis_size("tm")
    n_zl = lax.axis_size("z_lo")
    n_x = lax.axis_size("x")
    n_zh = lax.axis_size("z_hi")
    n_core = lax.axis_size("core")
    n_band = n_zh * n_core
    slots = pairs.shape[1]
    rows = nvec // (n_zl * n_x)
    width = 2 * nvec
    place = (lax.axis_index("tm") * n_zl + lax.axis_index("z_lo")) * n_x + lax.axis_index("x")
    base = (place * piece_len).astype(jnp.int32)
    smem = pl.BlockSpec(memory_space=pltpu.SMEM)
    vmem = pl.BlockSpec(memory_space=pltpu.VMEM)
    hbm = pl.BlockSpec(memory_space=pltpu.HBM)
    parts, chosen = pl.pallas_call(
        gram_kernel,
        in_specs=[smem, hbm, hbm, hbm, hbm],
        out_specs=[vmem, vmem],
        out_shape=[
            jax.ShapeDtypeStruct((n_tm * n_x, n_zl, rows, width), jnp.bfloat16),
            jax.ShapeDtypeStruct((slots, 2, nvec, nvec), jnp.bfloat16),
        ],
        scratch_shapes=[
            pltpu.VMEM((tcount, 2, colours, piece_len, nvec), jnp.bfloat16),
            pltpu.VMEM((tcount, colours, piece_len, width), jnp.bfloat16),
            pltpu.SMEM(mom.shape, jnp.int32),
            pltpu.SMEM(pairs.shape, jnp.int32),
            pltpu.SemaphoreType.DMA((tcount,)),
            pltpu.SemaphoreType.DMA((2,)),
            pltpu.SemaphoreType.DMA((slots,)),
        ],
        compiler_params=pltpu.CompilerParams(vmem_limit_bytes=16 << 20),
        name="gram",
    )(base.reshape(1), *(pltpu.with_memory_space_constraint(a, pltpu.HBM) for a in (mom, pairs, evecs, peram[0])))
    parts = lax.all_to_all(parts, ("x", "tm"), 0, 0, tiled=True)
    parts = pl.pallas_call(
        sum_kernel,
        in_specs=[vmem],
        out_specs=vmem,
        out_shape=jax.ShapeDtypeStruct((n_zh, n_zl, n_core, rows, width), jnp.bfloat16),
        compiler_params=pltpu.CompilerParams(vmem_limit_bytes=8 << 20),
        name="total",
    )(parts)
    parts = parts.reshape(n_band * n_zl, rows, width)
    parts = lax.all_to_all(parts, ("z_hi", "z_lo", "core"), 0, 0, tiled=True)
    meson, blocks = pl.pallas_call(
        block_kernel,
        in_specs=[smem, smem, vmem, vmem],
        out_specs=[hbm, hbm],
        out_shape=[
            jax.ShapeDtypeStruct((rows, 1, width), jnp.float32),
            jax.ShapeDtypeStruct((slots, rows, n_band, width), jnp.float32),
        ],
        scratch_shapes=[
            pltpu.VMEM((n_band, rows, width), jnp.float32),
            pltpu.VMEM((rows, 1, width), jnp.float32),
            pltpu.VMEM((slots, rows, n_band, width), jnp.float32),
            pltpu.SemaphoreType.DMA((slots + 1,)),
        ],
        compiler_params=pltpu.CompilerParams(vmem_limit_bytes=8 << 20),
        name="blocks",
    )(
        (lax.axis_index("z_hi") * n_core + lax.axis_index("core")).astype(jnp.int32).reshape(1),
        counts,
        parts.reshape(n_zh, n_zl, n_core, rows, width),
        chosen,
    )
    return meson[None], blocks[None]


def solution(mesh):
    n_tm, n_band, n_space = (mesh.shape[name] for name in ("tm", "band", "space"))
    fine = Mesh(
        mesh.devices.reshape(n_tm, n_band // CORES, CORES, Z_LO, n_space // Z_LO),
        ("tm", "z_hi", "core", "z_lo", "x"),
    )
    band = ("z_hi", "core")
    return jax.shard_map(
        per_device,
        mesh=fine,
        in_specs=(
            P(None, None, None, ("tm", "z_lo", "x"), None),
            P("tm", None, None, None, None),
            P(band, None),
            P(band, None),
            P(band),
        ),
        out_specs=(P("tm", ("z_lo", "x"), band, None), P("tm", band, ("z_lo", "x"), None, None)),
        check_vma=False,
    )
```

```python
import functools
import math

import jax
import jax.numpy as jnp
from jax import lax
from jax.experimental import pallas as pl
from jax.experimental.pallas import tpu as pltpu
from jax.sharding import Mesh, PartitionSpec as P

EXTENT = 64
Z_LO = 4
CORES = 2


def gram_kernel(
    base_ref, mom_hbm, evecs_hbm, out_ref, evecs_ref, right_ref, mom_ref, evecs_sems, mom_sem
):
    tcount, _, colours, sites, nvec = evecs_ref.shape
    n_x = out_ref.shape[0] // tcount
    n_zl, rows = out_ref.shape[1:3]
    mom_copy = pltpu.make_async_copy(mom_hbm, mom_ref, mom_sem)
    mom_copy.start()
    loads = [
        pltpu.make_async_copy(evecs_hbm.at[t], evecs_ref.at[t], evecs_sems.at[t]) for t in range(tcount)
    ]
    for copy in loads:
        copy.start()
    site = base_ref[0] + lax.broadcasted_iota(jnp.int32, (sites, nvec), 0)
    xs = site & (EXTENT - 1)
    ys = (site >> 6) & (EXTENT - 1)
    zs = site >> 12
    mom_copy.wait()
    wave = (mom_ref[0, 0] * xs + mom_ref[0, 1] * ys + mom_ref[0, 2] * zs) & (EXTENT - 1)
    theta = wave.astype(jnp.float32) * jnp.float32(2.0 * math.pi / EXTENT)
    cosine = jnp.cos(theta)
    sine = jnp.sin(theta)

    def rotate(t):
        for colour in range(colours):
            vreal = evecs_ref[t, 0, colour].astype(jnp.float32)
            vimag = evecs_ref[t, 1, colour].astype(jnp.float32)
            right_ref[t, colour, :, :nvec] = (cosine * vreal + sine * vimag).astype(jnp.bfloat16)
            right_ref[t, colour, :, nvec:] = (cosine * vimag - sine * vreal).astype(jnp.bfloat16)

    def multiply(t):
        right = right_ref[t].reshape(colours * sites, 2 * nvec)
        with_real, with_imag = (
            lax.dot_general(
                evecs_ref[t, part].reshape(colours * sites, nvec),
                right,
                (((0,), (0,)), ((), ())),
                preferred_element_type=jnp.float32,
            )
            for part in range(2)
        )
        meson = jnp.concatenate(
            [with_real[:, :nvec] + with_imag[:, nvec:], with_real[:, nvec:] - with_imag[:, :nvec]], axis=1
        ).astype(out_ref.dtype)
        for x in range(n_x):
            for zl in range(n_zl):
                first = (zl * n_x + x) * rows
                out_ref[x * tcount + t, zl] = meson[first : first + rows]

    groups = [list(range(4)), list(range(4, 8))]
    for g, group in enumerate(groups):
        for t in group:
            loads[t].wait()
        for t in group:
            rotate(t)
            multiply(t)


def sum_kernel(parts_ref, out_hbm, total_ref, sems):
    total_ref[...] = jnp.sum(parts_ref[...].astype(jnp.float32), axis=0).astype(jnp.bfloat16)
    copies = [
        pltpu.make_async_copy(total_ref, out_hbm.at[band], sems.at[band]) for band in range(out_hbm.shape[0])
    ]
    for copy in copies:
        copy.start()
    for copy in copies:
        copy.wait()


def pick_kernel(counts_ref, pairs_hbm, peram_hbm, out_ref, pairs_ref, pairs_sem, sems):
    nvec = peram_hbm.shape[-1]
    pairs_copy = pltpu.make_async_copy(pairs_hbm, pairs_ref, pairs_sem)
    pairs_copy.start()
    pairs_copy.wait()
    copies = [
        pltpu.make_async_copy(
            peram_hbm.at[pairs_ref[0, c]], out_ref.at[c // 2, :, :, pl.ds(c % 2 * nvec, nvec)], sems.at[c]
        )
        for c in range(pairs_ref.shape[1])
    ]
    for copy in copies:
        copy.start()
    for c, copy in enumerate(copies):
        copy.wait()

        @pl.when(c >= counts_ref[0])
        def _():
            out_ref[c // 2, :, :, c % 2 * nvec : (c % 2 + 1) * nvec] = jnp.zeros((2, nvec, nvec), out_ref.dtype)


def block_kernel(band_ref, parts_ref, chosen_ref, meson_hbm, out_hbm, total_ref, meson_ref, out_ref, sems):
    n_zh, cores, _, rows, width = parts_ref.shape
    moms = cores * n_zh
    slots = out_ref.shape[0]
    size = moms * rows
    nvec = width // 2
    for core in range(cores):
        for zh in range(n_zh):
            total_ref[zh * cores + core] = jnp.sum(parts_ref[zh, core].astype(jnp.float32), axis=0)
    own = total_ref[band_ref[0]]
    for row in range(rows):
        meson_ref[row] = own[row : row + 1]
    meson_copy = pltpu.make_async_copy(meson_ref, meson_hbm, sems.at[slots])
    meson_copy.start()
    left = jnp.swapaxes(total_ref[...], 0, 1).reshape(size, width)
    mreal = left[:, :nvec]
    mimag = left[:, nvec:]
    both = jnp.concatenate(
        [jnp.concatenate([mreal, -mimag], axis=1), jnp.concatenate([mimag, mreal], axis=1)], axis=0
    ).astype(jnp.bfloat16)
    copies = [meson_copy]
    for pair in range(slots // 2):
        right = chosen_ref[pair].reshape(width, 2 * nvec)
        prods = jnp.dot(both, right, preferred_element_type=jnp.float32)
        for q in range(2):
            c = 2 * pair + q
            prod = prods[:, q * nvec : (q + 1) * nvec]
            out_ref[c, :, :, :nvec] = prod[:size].reshape(rows, moms, nvec)
            out_ref[c, :, :, nvec:] = prod[size:].reshape(rows, moms, nvec)
            copies.append(pltpu.make_async_copy(out_ref.at[c], out_hbm.at[c], sems.at[c]))
            copies[-1].start()
    for copy in copies:
        copy.wait()


def per_device(evecs, peram, mom, pairs, counts):
    tcount, _, colours, piece_len, nvec = evecs.shape
    n_tm = lax.axis_size("tm")
    n_zl = lax.axis_size("z_lo")
    n_x = lax.axis_size("x")
    n_zh = lax.axis_size("z_hi")
    n_core = lax.axis_size("core")
    n_band = n_zh * n_core
    slots = pairs.shape[1]
    rows = nvec // (n_zl * n_x)
    width = 2 * nvec
    place = (lax.axis_index("tm") * n_zl + lax.axis_index("z_lo")) * n_x + lax.axis_index("x")
    base = (place * piece_len).astype(jnp.int32)
    hold = functools.partial(pltpu.with_memory_space_constraint, memory_space=pltpu.HBM)
    smem = pl.BlockSpec(memory_space=pltpu.SMEM)
    vmem = pl.BlockSpec(memory_space=pltpu.VMEM)
    hbm = pl.BlockSpec(memory_space=pltpu.HBM)
    parts = pl.pallas_call(
        gram_kernel,
        in_specs=[smem, hbm, hbm],
        out_specs=vmem,
        out_shape=jax.ShapeDtypeStruct((n_tm * n_x, n_zl, rows, width), jnp.bfloat16),
        scratch_shapes=[
            pltpu.VMEM((tcount, 2, colours, piece_len, nvec), jnp.bfloat16),
            pltpu.VMEM((tcount, colours, piece_len, width), jnp.bfloat16),
            pltpu.SMEM(mom.shape, jnp.int32),
            pltpu.SemaphoreType.DMA((tcount,)),
            pltpu.SemaphoreType.DMA,
        ],
        compiler_params=pltpu.CompilerParams(vmem_limit_bytes=16 << 20),
        name="gram",
    )(base.reshape(1), hold(mom), hold(evecs))
    parts = lax.all_to_all(parts, ("x", "tm"), 0, 0, tiled=True)
    parts = pl.pallas_call(
        sum_kernel,
        in_specs=[vmem],
        out_specs=hbm,
        out_shape=jax.ShapeDtypeStruct((n_band, n_zl, rows, width), jnp.bfloat16),
        scratch_shapes=[pltpu.VMEM((n_zl, rows, width), jnp.bfloat16), pltpu.SemaphoreType.DMA((n_band,))],
        compiler_params=pltpu.CompilerParams(vmem_limit_bytes=8 << 20),
        name="total",
    )(parts)
    parts = parts.reshape(n_band * n_zl, rows, width)
    parts = lax.all_to_all(parts, ("z_hi", "core", "z_lo"), 0, 0, tiled=True)
    chosen = pl.pallas_call(
        pick_kernel,
        in_specs=[smem, hbm, hbm],
        out_specs=vmem,
        out_shape=jax.ShapeDtypeStruct((slots // 2, 2, nvec, 2 * nvec), jnp.bfloat16),
        scratch_shapes=[
            pltpu.SMEM(pairs.shape, jnp.int32),
            pltpu.SemaphoreType.DMA,
            pltpu.SemaphoreType.DMA((slots,)),
        ],
        compiler_params=pltpu.CompilerParams(vmem_limit_bytes=8 << 20),
        cost_estimate=pl.CostEstimate(flops=0, transcendentals=0, bytes_accessed=8 * slots * nvec * nvec),
        name="pick",
    )(counts, hold(pairs), hold(peram[0]))
    meson, blocks = pl.pallas_call(
        block_kernel,
        in_specs=[smem, vmem, vmem],
        out_specs=[hbm, hbm],
        out_shape=[
            jax.ShapeDtypeStruct((rows, 1, width), jnp.float32),
            jax.ShapeDtypeStruct((slots, rows, n_band, width), jnp.float32),
        ],
        scratch_shapes=[
            pltpu.VMEM((n_band, rows, width), jnp.float32),
            pltpu.VMEM((rows, 1, width), jnp.float32),
            pltpu.VMEM((slots, rows, n_band, width), jnp.float32),
            pltpu.SemaphoreType.DMA((slots + 1,)),
        ],
        compiler_params=pltpu.CompilerParams(vmem_limit_bytes=8 << 20),
        name="blocks",
    )(
        (lax.axis_index("z_hi") * n_core + lax.axis_index("core")).astype(jnp.int32).reshape(1),
        parts.reshape(n_zh, n_core, n_zl, rows, width),
        chosen,
    )
    return meson[None], blocks[None]


def solution(mesh):
    n_tm, n_band, n_space = (mesh.shape[name] for name in ("tm", "band", "space"))
    fine = Mesh(
        mesh.devices.reshape(n_tm, n_band // CORES, CORES, Z_LO, n_space // Z_LO),
        ("tm", "z_hi", "core", "z_lo", "x"),
    )
    band = ("z_hi", "core")
    return jax.shard_map(
        per_device,
        mesh=fine,
        in_specs=(
            P(None, None, None, ("tm", "z_lo", "x"), None),
            P("tm", None, None, None, None),
            P(band, None),
            P(band, None),
            P(band),
        ),
        out_specs=(P("tm", ("z_lo", "x"), band, None), P("tm", band, ("z_lo", "x"), None, None)),
        check_vma=False,
    )
```

```python
import functools
import math

import jax
import jax.numpy as jnp
from jax import lax
from jax.experimental import pallas as pl
from jax.experimental.pallas import tpu as pltpu
from jax.sharding import Mesh, PartitionSpec as P

EXTENT = 64
Z_LO = 4
CORES = 2


def gram_kernel(
    base_ref, mom_hbm, evecs_hbm, out_ref, evecs_ref, right_ref, mom_ref, evecs_sems, mom_sem
):
    tcount, _, colours, sites, nvec = evecs_ref.shape
    n_x = out_ref.shape[0] // tcount
    n_zl, rows = out_ref.shape[1:3]
    mom_copy = pltpu.make_async_copy(mom_hbm, mom_ref, mom_sem)
    mom_copy.start()
    loads = [
        pltpu.make_async_copy(evecs_hbm.at[t], evecs_ref.at[t], evecs_sems.at[t]) for t in range(tcount)
    ]
    for copy in loads:
        copy.start()
    site = base_ref[0] + lax.broadcasted_iota(jnp.int32, (sites, nvec), 0)
    xs = site & (EXTENT - 1)
    ys = (site >> 6) & (EXTENT - 1)
    zs = site >> 12
    mom_copy.wait()
    wave = (mom_ref[0, 0] * xs + mom_ref[0, 1] * ys + mom_ref[0, 2] * zs) & (EXTENT - 1)
    theta = wave.astype(jnp.float32) * jnp.float32(2.0 * math.pi / EXTENT)
    cosine = jnp.cos(theta)
    sine = jnp.sin(theta)

    def rotate(t):
        for colour in range(colours):
            vreal = evecs_ref[t, 0, colour].astype(jnp.float32)
            vimag = evecs_ref[t, 1, colour].astype(jnp.float32)
            right_ref[t, colour, :, :nvec] = (cosine * vreal + sine * vimag).astype(jnp.bfloat16)
            right_ref[t, colour, :, nvec:] = (cosine * vimag - sine * vreal).astype(jnp.bfloat16)

    def multiply(t):
        right = right_ref[t].reshape(colours * sites, 2 * nvec)
        with_real, with_imag = (
            lax.dot_general(
                evecs_ref[t, part].reshape(colours * sites, nvec),
                right,
                (((0,), (0,)), ((), ())),
                preferred_element_type=jnp.float32,
            )
            for part in range(2)
        )
        meson = jnp.concatenate(
            [with_real[:, :nvec] + with_imag[:, nvec:], with_real[:, nvec:] - with_imag[:, :nvec]], axis=1
        ).astype(out_ref.dtype)
        for x in range(n_x):
            for zl in range(n_zl):
                first = (zl * n_x + x) * rows
                out_ref[x * tcount + t, zl] = meson[first : first + rows]

    groups = [list(range(4)), list(range(4, 8))]
    for g, group in enumerate(groups):
        for t in group:
            loads[t].wait()
        for t in group:
            rotate(t)
            multiply(t)


def sum_kernel(parts_ref, out_hbm, total_ref, sems):
    total_ref[...] = jnp.sum(parts_ref[...].astype(jnp.float32), axis=0).astype(jnp.bfloat16)
    copies = [
        pltpu.make_async_copy(total_ref, out_hbm.at[band], sems.at[band]) for band in range(out_hbm.shape[0])
    ]
    for copy in copies:
        copy.start()
    for copy in copies:
        copy.wait()


def pick_kernel(counts_ref, pairs_hbm, peram_hbm, out_ref, pairs_ref, pairs_sem, sems):
    nvec = peram_hbm.shape[-1]
    pairs_copy = pltpu.make_async_copy(pairs_hbm, pairs_ref, pairs_sem)
    pairs_copy.start()
    pairs_copy.wait()
    copies = [
        pltpu.make_async_copy(
            peram_hbm.at[pairs_ref[0, c]], out_ref.at[c // 2, :, :, pl.ds(c % 2 * nvec, nvec)], sems.at[c]
        )
        for c in range(pairs_ref.shape[1])
    ]
    for copy in copies:
        copy.start()
    for c, copy in enumerate(copies):
        copy.wait()

        @pl.when(c >= counts_ref[0])
        def _():
            out_ref[c // 2, :, :, c % 2 * nvec : (c % 2 + 1) * nvec] = jnp.zeros((2, nvec, nvec), out_ref.dtype)


def block_kernel(band_ref, parts_ref, chosen_ref, meson_hbm, out_hbm, total_ref, meson_ref, out_ref, sems):
    n_zh, cores, _, rows, width = parts_ref.shape
    moms = cores * n_zh
    slots = out_ref.shape[0]
    size = moms * rows
    nvec = width // 2
    for core in range(cores):
        for zh in range(n_zh):
            total_ref[zh * cores + core] = jnp.sum(parts_ref[zh, core].astype(jnp.float32), axis=0)
    own = total_ref[band_ref[0]]
    for row in range(rows):
        meson_ref[row] = own[row : row + 1]
    meson_copy = pltpu.make_async_copy(meson_ref, meson_hbm, sems.at[slots])
    meson_copy.start()
    left = jnp.swapaxes(total_ref[...], 0, 1).reshape(size, width)
    mreal = left[:, :nvec]
    mimag = left[:, nvec:]
    both = jnp.concatenate(
        [jnp.concatenate([mreal, -mimag], axis=1), jnp.concatenate([mimag, mreal], axis=1)], axis=0
    ).astype(jnp.bfloat16)
    copies = [meson_copy]
    for pair in range(slots // 2):
        right = chosen_ref[pair].reshape(width, 2 * nvec)
        prods = jnp.dot(both, right, preferred_element_type=jnp.float32)
        for q in range(2):
            c = 2 * pair + q
            prod = prods[:, q * nvec : (q + 1) * nvec]
            out_ref[c, :, :, :nvec] = prod[:size].reshape(rows, moms, nvec)
            out_ref[c, :, :, nvec:] = prod[size:].reshape(rows, moms, nvec)
            copies.append(pltpu.make_async_copy(out_ref.at[c], out_hbm.at[c], sems.at[c]))
            copies[-1].start()
    for copy in copies:
        copy.wait()


def per_device(evecs, peram, mom, pairs, counts):
    tcount, _, colours, piece_len, nvec = evecs.shape
    n_tm = lax.axis_size("tm")
    n_zl = lax.axis_size("z_lo")
    n_x = lax.axis_size("x")
    n_zh = lax.axis_size("z_hi")
    n_core = lax.axis_size("core")
    n_band = n_zh * n_core
    slots = pairs.shape[1]
    rows = nvec // (n_zl * n_x)
    width = 2 * nvec
    place = (lax.axis_index("tm") * n_zl + lax.axis_index("z_lo")) * n_x + lax.axis_index("x")
    base = (place * piece_len).astype(jnp.int32)
    hold = functools.partial(pltpu.with_memory_space_constraint, memory_space=pltpu.HBM)
    smem = pl.BlockSpec(memory_space=pltpu.SMEM)
    vmem = pl.BlockSpec(memory_space=pltpu.VMEM)
    hbm = pl.BlockSpec(memory_space=pltpu.HBM)
    parts = pl.pallas_call(
        gram_kernel,
        in_specs=[smem, hbm, hbm],
        out_specs=vmem,
        out_shape=jax.ShapeDtypeStruct((n_tm * n_x, n_zl, rows, width), jnp.bfloat16),
        scratch_shapes=[
            pltpu.VMEM((tcount, 2, colours, piece_len, nvec), jnp.bfloat16),
            pltpu.VMEM((tcount, colours, piece_len, width), jnp.bfloat16),
            pltpu.SMEM(mom.shape, jnp.int32),
            pltpu.SemaphoreType.DMA((tcount,)),
            pltpu.SemaphoreType.DMA,
        ],
        compiler_params=pltpu.CompilerParams(vmem_limit_bytes=16 << 20),
        name="gram",
    )(base.reshape(1), hold(mom), hold(evecs))
    parts = parts.reshape(n_tm * n_x, n_zl * rows, width)
    parts = lax.all_to_all(parts, ("x", "tm"), 0, 0, tiled=True)
    parts = parts.reshape(n_tm * n_x, n_zl, rows, width)
    parts = pl.pallas_call(
        sum_kernel,
        in_specs=[vmem],
        out_specs=hbm,
        out_shape=jax.ShapeDtypeStruct((n_band, n_zl, rows, width), jnp.bfloat16),
        scratch_shapes=[pltpu.VMEM((n_zl, rows, width), jnp.bfloat16), pltpu.SemaphoreType.DMA((n_band,))],
        compiler_params=pltpu.CompilerParams(vmem_limit_bytes=8 << 20),
        name="total",
    )(parts)
    parts = parts.reshape(n_band * n_zl, rows, width)
    parts = lax.all_to_all(parts, ("z_hi", "core", "z_lo"), 0, 0, tiled=True)
    chosen = pl.pallas_call(
        pick_kernel,
        in_specs=[smem, hbm, hbm],
        out_specs=vmem,
        out_shape=jax.ShapeDtypeStruct((slots // 2, 2, nvec, 2 * nvec), jnp.bfloat16),
        scratch_shapes=[
            pltpu.SMEM(pairs.shape, jnp.int32),
            pltpu.SemaphoreType.DMA,
            pltpu.SemaphoreType.DMA((slots,)),
        ],
        compiler_params=pltpu.CompilerParams(vmem_limit_bytes=8 << 20),
        cost_estimate=pl.CostEstimate(flops=0, transcendentals=0, bytes_accessed=8 * slots * nvec * nvec),
        name="pick",
    )(counts, hold(pairs), hold(peram[0]))
    meson, blocks = pl.pallas_call(
        block_kernel,
        in_specs=[smem, vmem, vmem],
        out_specs=[hbm, hbm],
        out_shape=[
            jax.ShapeDtypeStruct((rows, 1, width), jnp.float32),
            jax.ShapeDtypeStruct((slots, rows, n_band, width), jnp.float32),
        ],
        scratch_shapes=[
            pltpu.VMEM((n_band, rows, width), jnp.float32),
            pltpu.VMEM((rows, 1, width), jnp.float32),
            pltpu.VMEM((slots, rows, n_band, width), jnp.float32),
            pltpu.SemaphoreType.DMA((slots + 1,)),
        ],
        compiler_params=pltpu.CompilerParams(vmem_limit_bytes=8 << 20),
        name="blocks",
    )(
        (lax.axis_index("z_hi") * n_core + lax.axis_index("core")).astype(jnp.int32).reshape(1),
        parts.reshape(n_zh, n_core, n_zl, rows, width),
        chosen,
    )
    return meson[None], blocks[None]


def solution(mesh):
    n_tm, n_band, n_space = (mesh.shape[name] for name in ("tm", "band", "space"))
    fine = Mesh(
        mesh.devices.reshape(n_tm, n_band // CORES, CORES, Z_LO, n_space // Z_LO),
        ("tm", "z_hi", "core", "z_lo", "x"),
    )
    band = ("z_hi", "core")
    return jax.shard_map(
        per_device,
        mesh=fine,
        in_specs=(
            P(None, None, None, ("tm", "z_lo", "x"), None),
            P("tm", None, None, None, None),
            P(band, None),
            P(band, None),
            P(band),
        ),
        out_specs=(P("tm", ("z_lo", "x"), band, None), P("tm", band, ("z_lo", "x"), None, None)),
        check_vma=False,
    )
```

```python
import math

import jax
import jax.numpy as jnp
from jax import lax
from jax.experimental import pallas as pl
from jax.experimental.pallas import tpu as pltpu
from jax.sharding import Mesh, PartitionSpec as P

EXTENT = 64
Z_LO = 4
CORES = 2


def gram_kernel(
    base_ref, _, live_ref, mom_hbm, pairs_hbm, evecs_hbm, peram_hbm, out_ref, chosen_ref,
    evecs_ref, right_ref, mom_ref, pairs_ref, evecs_sems, small_sems, pick_sems,
):
    tcount, _, colours, sites, nvec = evecs_ref.shape
    slots = chosen_ref.shape[0]
    n_x = out_ref.shape[0] // tcount
    n_zl, rows = out_ref.shape[1:3]
    small = [
        pltpu.make_async_copy(mom_hbm, mom_ref, small_sems.at[0]),
        pltpu.make_async_copy(pairs_hbm, pairs_ref, small_sems.at[1]),
    ]
    loads = [
        pltpu.make_async_copy(evecs_hbm.at[t], evecs_ref.at[t], evecs_sems.at[t]) for t in range(tcount)
    ]
    for copy in small + loads:
        copy.start()
    site = base_ref[0] + lax.broadcasted_iota(jnp.int32, (sites, nvec), 0)
    xs = site & (EXTENT - 1)
    ys = (site >> 6) & (EXTENT - 1)
    zs = site >> 12
    for copy in small:
        copy.wait()
    picks = [
        pltpu.make_async_copy(peram_hbm.at[pairs_ref[0, c]], chosen_ref.at[c], pick_sems.at[c])
        for c in range(slots)
    ]
    for copy in picks:
        copy.start()
    wave = (mom_ref[0, 0] * xs + mom_ref[0, 1] * ys + mom_ref[0, 2] * zs) & (EXTENT - 1)
    theta = wave.astype(jnp.float32) * jnp.float32(2.0 * math.pi / EXTENT)
    cosine = jnp.cos(theta)
    sine = jnp.sin(theta)

    def rotate(t):
        for colour in range(colours):
            vreal = evecs_ref[t, 0, colour].astype(jnp.float32)
            vimag = evecs_ref[t, 1, colour].astype(jnp.float32)
            right_ref[t, colour, :, :nvec] = (cosine * vreal + sine * vimag).astype(jnp.bfloat16)
            right_ref[t, colour, :, nvec:] = (cosine * vimag - sine * vreal).astype(jnp.bfloat16)

    def multiply(t):
        right = right_ref[t].reshape(colours * sites, 2 * nvec)
        with_real, with_imag = (
            lax.dot_general(
                evecs_ref[t, part].reshape(colours * sites, nvec),
                right,
                (((0,), (0,)), ((), ())),
                preferred_element_type=jnp.float32,
            )
            for part in range(2)
        )
        meson = jnp.concatenate(
            [with_real[:, :nvec] + with_imag[:, nvec:], with_real[:, nvec:] - with_imag[:, :nvec]], axis=1
        ).astype(out_ref.dtype)
        for x in range(n_x):
            for zl in range(n_zl):
                first = (zl * n_x + x) * rows
                out_ref[x * tcount + t, zl] = meson[first : first + rows]

    groups = [list(range(4)), list(range(4, 8))]
    for g, group in enumerate(groups):
        for t in group:
            loads[t].wait()
        for t in group:
            rotate(t)
            multiply(t)
    for c, copy in enumerate(picks):
        copy.wait()

        @pl.when(c >= live_ref[0])
        def _():
            chosen_ref[c] = jnp.zeros(chosen_ref.shape[1:], chosen_ref.dtype)


def sum_kernel(parts_ref, out_ref):
    total = jnp.sum(parts_ref[...].astype(jnp.float32), axis=0).astype(jnp.bfloat16)
    for band in range(out_ref.shape[0]):
        out_ref[band] = total


def block_kernel(band_ref, parts_ref, chosen_ref, meson_hbm, out_hbm, total_ref, meson_ref, out_ref, sems):
    n_zh, cores, _, rows, width = parts_ref.shape
    moms = cores * n_zh
    slots = out_ref.shape[0]
    size = moms * rows
    nvec = width // 2
    for core in range(cores):
        for zh in range(n_zh):
            total_ref[zh * cores + core] = jnp.sum(parts_ref[zh, core].astype(jnp.float32), axis=0)
    own = total_ref[band_ref[0]]
    for row in range(rows):
        meson_ref[row] = own[row : row + 1]
    meson_copy = pltpu.make_async_copy(meson_ref, meson_hbm, sems.at[slots])
    meson_copy.start()
    left = jnp.swapaxes(total_ref[...], 0, 1).reshape(size, width)
    mreal = left[:, :nvec]
    mimag = left[:, nvec:]
    both = jnp.concatenate(
        [jnp.concatenate([mreal, -mimag], axis=1), jnp.concatenate([mimag, mreal], axis=1)], axis=0
    ).astype(jnp.bfloat16)
    copies = [meson_copy]
    for pair in range(slots // 2):
        right = jnp.concatenate([chosen_ref[2 * pair + q].reshape(width, nvec) for q in range(2)], axis=1)
        prods = jnp.dot(both, right, preferred_element_type=jnp.float32)
        for q in range(2):
            c = 2 * pair + q
            prod = prods[:, q * nvec : (q + 1) * nvec]
            out_ref[c, :, :, :nvec] = prod[:size].reshape(rows, moms, nvec)
            out_ref[c, :, :, nvec:] = prod[size:].reshape(rows, moms, nvec)
            copies.append(pltpu.make_async_copy(out_ref.at[c], out_hbm.at[c], sems.at[c]))
            copies[-1].start()
    for copy in copies:
        copy.wait()


def per_device(evecs, peram, mom, pairs, counts):
    tcount, _, colours, piece_len, nvec = evecs.shape
    n_tm = lax.axis_size("tm")
    n_zl = lax.axis_size("z_lo")
    n_x = lax.axis_size("x")
    n_zh = lax.axis_size("z_hi")
    n_core = lax.axis_size("core")
    n_band = n_zh * n_core
    slots = pairs.shape[1]
    rows = nvec // (n_zl * n_x)
    width = 2 * nvec
    place = (lax.axis_index("tm") * n_zl + lax.axis_index("z_lo")) * n_x + lax.axis_index("x")
    base = (place * piece_len).astype(jnp.int32)
    band = (lax.axis_index("z_hi") * n_core + lax.axis_index("core")).astype(jnp.int32).reshape(1)
    smem = pl.BlockSpec(memory_space=pltpu.SMEM)
    vmem = pl.BlockSpec(memory_space=pltpu.VMEM)
    hbm = pl.BlockSpec(memory_space=pltpu.HBM)
    parts, chosen = pl.pallas_call(
        gram_kernel,
        in_specs=[smem, smem, smem, hbm, hbm, hbm, hbm],
        out_specs=[vmem, vmem],
        out_shape=[
            jax.ShapeDtypeStruct((n_tm * n_x, n_zl, rows, width), jnp.bfloat16),
            jax.ShapeDtypeStruct((slots, 2, nvec, nvec), jnp.bfloat16),
        ],
        scratch_shapes=[
            pltpu.VMEM((tcount, 2, colours, piece_len, nvec), jnp.bfloat16),
            pltpu.VMEM((tcount, colours, piece_len, width), jnp.bfloat16),
            pltpu.SMEM(mom.shape, jnp.int32),
            pltpu.SMEM(pairs.shape, jnp.int32),
            pltpu.SemaphoreType.DMA((tcount,)),
            pltpu.SemaphoreType.DMA((2,)),
            pltpu.SemaphoreType.DMA((slots,)),
        ],
        compiler_params=pltpu.CompilerParams(vmem_limit_bytes=16 << 20),
        name="gram",
    )(base.reshape(1), band, counts, *(pltpu.with_memory_space_constraint(a, pltpu.HBM) for a in (mom, pairs, evecs, peram[0])))
    parts = parts.reshape(n_tm * n_x, n_zl * rows, width)
    parts = lax.all_to_all(parts, ("x", "tm"), 0, 0, tiled=True)
    parts = parts.reshape(n_tm * n_x, n_zl, rows, width)
    parts = pl.pallas_call(
        sum_kernel,
        in_specs=[vmem],
        out_specs=vmem,
        out_shape=jax.ShapeDtypeStruct((n_band, n_zl, rows, width), jnp.bfloat16),
        compiler_params=pltpu.CompilerParams(vmem_limit_bytes=8 << 20),
        name="total",
    )(parts)
    parts = parts.reshape(n_band * n_zl, rows, width)
    parts = lax.all_to_all(parts, ("z_hi", "core", "z_lo"), 0, 0, tiled=True)
    meson, blocks = pl.pallas_call(
        block_kernel,
        in_specs=[smem, vmem, vmem],
        out_specs=[hbm, hbm],
        out_shape=[
            jax.ShapeDtypeStruct((rows, 1, width), jnp.float32),
            jax.ShapeDtypeStruct((slots, rows, n_band, width), jnp.float32),
        ],
        scratch_shapes=[
            pltpu.VMEM((n_band, rows, width), jnp.float32),
            pltpu.VMEM((rows, 1, width), jnp.float32),
            pltpu.VMEM((slots, rows, n_band, width), jnp.float32),
            pltpu.SemaphoreType.DMA((slots + 1,)),
        ],
        compiler_params=pltpu.CompilerParams(vmem_limit_bytes=8 << 20),
        name="blocks",
    )(
        band,
        parts.reshape(n_zh, n_core, n_zl, rows, width),
        chosen,
    )
    return meson[None], blocks[None]


def solution(mesh):
    n_tm, n_band, n_space = (mesh.shape[name] for name in ("tm", "band", "space"))
    fine = Mesh(
        mesh.devices.reshape(n_tm, n_band // CORES, CORES, Z_LO, n_space // Z_LO),
        ("tm", "z_hi", "core", "z_lo", "x"),
    )
    band = ("z_hi", "core")
    return jax.shard_map(
        per_device,
        mesh=fine,
        in_specs=(
            P(None, None, None, ("tm", "z_lo", "x"), None),
            P("tm", None, None, None, None),
            P(band, None),
            P(band, None),
            P(band),
        ),
        out_specs=(P("tm", ("z_lo", "x"), band, None), P("tm", band, ("z_lo", "x"), None, None)),
        check_vma=False,
    )
```

```python
import functools
import math

import jax
import jax.numpy as jnp
from jax import lax
from jax.experimental import pallas as pl
from jax.experimental.pallas import tpu as pltpu
from jax.sharding import Mesh, PartitionSpec as P

EXTENT = 64
Z_LO = 4
CORES = 2


def gram_kernel(
    base_ref, mom_hbm, evecs_hbm, out_ref, evecs_ref, right_ref, mom_ref, evecs_sems, mom_sem
):
    tcount, _, colours, sites, nvec = evecs_ref.shape
    n_x = out_ref.shape[0] // tcount
    n_zl, rows = out_ref.shape[1:3]
    mom_copy = pltpu.make_async_copy(mom_hbm, mom_ref, mom_sem)
    mom_copy.start()
    loads = [
        pltpu.make_async_copy(evecs_hbm.at[t], evecs_ref.at[t], evecs_sems.at[t]) for t in range(tcount)
    ]
    for copy in loads:
        copy.start()
    site = base_ref[0] + lax.broadcasted_iota(jnp.int32, (sites, nvec), 0)
    xs = site & (EXTENT - 1)
    ys = (site >> 6) & (EXTENT - 1)
    zs = site >> 12
    mom_copy.wait()
    wave = (mom_ref[0, 0] * xs + mom_ref[0, 1] * ys + mom_ref[0, 2] * zs) & (EXTENT - 1)
    theta = wave.astype(jnp.float32) * jnp.float32(2.0 * math.pi / EXTENT)
    cosine = jnp.cos(theta)
    sine = jnp.sin(theta)

    def rotate(t):
        for colour in range(colours):
            vreal = evecs_ref[t, 0, colour].astype(jnp.float32)
            vimag = evecs_ref[t, 1, colour].astype(jnp.float32)
            right_ref[t, colour, :, :nvec] = (cosine * vreal + sine * vimag).astype(jnp.bfloat16)
            right_ref[t, colour, :, nvec:] = (cosine * vimag - sine * vreal).astype(jnp.bfloat16)

    def multiply(t):
        right = right_ref[t].reshape(colours * sites, 2 * nvec)
        with_real, with_imag = (
            sum(
                lax.dot_general(
                    evecs_ref[t, part, colour],
                    right_ref[t, colour],
                    (((0,), (0,)), ((), ())),
                    preferred_element_type=jnp.float32,
                )
                for colour in range(colours)
            )
            for part in range(2)
        )
        meson = jnp.concatenate(
            [with_real[:, :nvec] + with_imag[:, nvec:], with_real[:, nvec:] - with_imag[:, :nvec]], axis=1
        ).astype(out_ref.dtype)
        for x in range(n_x):
            for zl in range(n_zl):
                first = (zl * n_x + x) * rows
                out_ref[x * tcount + t, zl] = meson[first : first + rows]

    groups = [list(range(4)), list(range(4, 8))]
    for g, group in enumerate(groups):
        for t in group:
            loads[t].wait()
        for t in group:
            rotate(t)
            multiply(t)


def sum_kernel(parts_ref, out_hbm, total_ref, sems):
    total_ref[...] = jnp.sum(parts_ref[...].astype(jnp.float32), axis=0).astype(jnp.bfloat16)
    copies = [
        pltpu.make_async_copy(total_ref, out_hbm.at[band], sems.at[band]) for band in range(out_hbm.shape[0])
    ]
    for copy in copies:
        copy.start()
    for copy in copies:
        copy.wait()


def pick_kernel(counts_ref, pairs_hbm, peram_hbm, out_ref, pairs_ref, pairs_sem, sems):
    nvec = peram_hbm.shape[-1]
    pairs_copy = pltpu.make_async_copy(pairs_hbm, pairs_ref, pairs_sem)
    pairs_copy.start()
    pairs_copy.wait()
    copies = [
        pltpu.make_async_copy(
            peram_hbm.at[pairs_ref[0, c]], out_ref.at[c // 2, :, :, pl.ds(c % 2 * nvec, nvec)], sems.at[c]
        )
        for c in range(pairs_ref.shape[1])
    ]
    for copy in copies:
        copy.start()
    for c, copy in enumerate(copies):
        copy.wait()

        @pl.when(c >= counts_ref[0])
        def _():
            out_ref[c // 2, :, :, c % 2 * nvec : (c % 2 + 1) * nvec] = jnp.zeros((2, nvec, nvec), out_ref.dtype)


def block_kernel(band_ref, parts_ref, chosen_ref, meson_hbm, out_hbm, total_ref, meson_ref, out_ref, sems):
    n_zh, cores, _, rows, width = parts_ref.shape
    moms = cores * n_zh
    slots = out_ref.shape[0]
    size = moms * rows
    nvec = width // 2
    for core in range(cores):
        for zh in range(n_zh):
            total_ref[zh * cores + core] = jnp.sum(parts_ref[zh, core].astype(jnp.float32), axis=0)
    own = total_ref[band_ref[0]]
    for row in range(rows):
        meson_ref[row] = own[row : row + 1]
    meson_copy = pltpu.make_async_copy(meson_ref, meson_hbm, sems.at[slots])
    meson_copy.start()
    left = jnp.swapaxes(total_ref[...], 0, 1).reshape(size, width)
    mreal = left[:, :nvec]
    mimag = left[:, nvec:]
    both = jnp.concatenate(
        [jnp.concatenate([mreal, -mimag], axis=1), jnp.concatenate([mimag, mreal], axis=1)], axis=0
    ).astype(jnp.bfloat16)
    copies = [meson_copy]
    for pair in range(slots // 2):
        right = chosen_ref[pair].reshape(width, 2 * nvec)
        prods = jnp.dot(both, right, preferred_element_type=jnp.float32)
        for q in range(2):
            c = 2 * pair + q
            prod = prods[:, q * nvec : (q + 1) * nvec]
            out_ref[c, :, :, :nvec] = prod[:size].reshape(rows, moms, nvec)
            out_ref[c, :, :, nvec:] = prod[size:].reshape(rows, moms, nvec)
            copies.append(pltpu.make_async_copy(out_ref.at[c], out_hbm.at[c], sems.at[c]))
            copies[-1].start()
    for copy in copies:
        copy.wait()


def per_device(evecs, peram, mom, pairs, counts):
    tcount, _, colours, piece_len, nvec = evecs.shape
    n_tm = lax.axis_size("tm")
    n_zl = lax.axis_size("z_lo")
    n_x = lax.axis_size("x")
    n_zh = lax.axis_size("z_hi")
    n_core = lax.axis_size("core")
    n_band = n_zh * n_core
    slots = pairs.shape[1]
    rows = nvec // (n_zl * n_x)
    width = 2 * nvec
    place = (lax.axis_index("tm") * n_zl + lax.axis_index("z_lo")) * n_x + lax.axis_index("x")
    base = (place * piece_len).astype(jnp.int32)
    hold = functools.partial(pltpu.with_memory_space_constraint, memory_space=pltpu.HBM)
    smem = pl.BlockSpec(memory_space=pltpu.SMEM)
    vmem = pl.BlockSpec(memory_space=pltpu.VMEM)
    hbm = pl.BlockSpec(memory_space=pltpu.HBM)
    parts = pl.pallas_call(
        gram_kernel,
        in_specs=[smem, hbm, hbm],
        out_specs=vmem,
        out_shape=jax.ShapeDtypeStruct((n_tm * n_x, n_zl, rows, width), jnp.bfloat16),
        scratch_shapes=[
            pltpu.VMEM((tcount, 2, colours, piece_len, nvec), jnp.bfloat16),
            pltpu.VMEM((tcount, colours, piece_len, width), jnp.bfloat16),
            pltpu.SMEM(mom.shape, jnp.int32),
            pltpu.SemaphoreType.DMA((tcount,)),
            pltpu.SemaphoreType.DMA,
        ],
        compiler_params=pltpu.CompilerParams(vmem_limit_bytes=16 << 20),
        name="gram",
    )(base.reshape(1), hold(mom), hold(evecs))
    parts = parts.reshape(n_tm * n_x, n_zl * rows, width)
    parts = lax.all_to_all(parts, ("x", "tm"), 0, 0, tiled=True)
    parts = parts.reshape(n_tm * n_x, n_zl, rows, width)
    parts = pl.pallas_call(
        sum_kernel,
        in_specs=[vmem],
        out_specs=hbm,
        out_shape=jax.ShapeDtypeStruct((n_band, n_zl, rows, width), jnp.bfloat16),
        scratch_shapes=[pltpu.VMEM((n_zl, rows, width), jnp.bfloat16), pltpu.SemaphoreType.DMA((n_band,))],
        compiler_params=pltpu.CompilerParams(vmem_limit_bytes=8 << 20),
        name="total",
    )(parts)
    parts = parts.reshape(n_band * n_zl, rows, width)
    parts = lax.all_to_all(parts, ("z_hi", "core", "z_lo"), 0, 0, tiled=True)
    chosen = pl.pallas_call(
        pick_kernel,
        in_specs=[smem, hbm, hbm],
        out_specs=vmem,
        out_shape=jax.ShapeDtypeStruct((slots // 2, 2, nvec, 2 * nvec), jnp.bfloat16),
        scratch_shapes=[
            pltpu.SMEM(pairs.shape, jnp.int32),
            pltpu.SemaphoreType.DMA,
            pltpu.SemaphoreType.DMA((slots,)),
        ],
        compiler_params=pltpu.CompilerParams(vmem_limit_bytes=8 << 20),
        cost_estimate=pl.CostEstimate(flops=0, transcendentals=0, bytes_accessed=8 * slots * nvec * nvec),
        name="pick",
    )(counts, hold(pairs), hold(peram[0]))
    meson, blocks = pl.pallas_call(
        block_kernel,
        in_specs=[smem, vmem, vmem],
        out_specs=[hbm, hbm],
        out_shape=[
            jax.ShapeDtypeStruct((rows, 1, width), jnp.float32),
            jax.ShapeDtypeStruct((slots, rows, n_band, width), jnp.float32),
        ],
        scratch_shapes=[
            pltpu.VMEM((n_band, rows, width), jnp.float32),
            pltpu.VMEM((rows, 1, width), jnp.float32),
            pltpu.VMEM((slots, rows, n_band, width), jnp.float32),
            pltpu.SemaphoreType.DMA((slots + 1,)),
        ],
        compiler_params=pltpu.CompilerParams(vmem_limit_bytes=8 << 20),
        name="blocks",
    )(
        (lax.axis_index("z_hi") * n_core + lax.axis_index("core")).astype(jnp.int32).reshape(1),
        parts.reshape(n_zh, n_core, n_zl, rows, width),
        chosen,
    )
    return meson[None], blocks[None]


def solution(mesh):
    n_tm, n_band, n_space = (mesh.shape[name] for name in ("tm", "band", "space"))
    fine = Mesh(
        mesh.devices.reshape(n_tm, n_band // CORES, CORES, Z_LO, n_space // Z_LO),
        ("tm", "z_hi", "core", "z_lo", "x"),
    )
    band = ("z_hi", "core")
    return jax.shard_map(
        per_device,
        mesh=fine,
        in_specs=(
            P(None, None, None, ("tm", "z_lo", "x"), None),
            P("tm", None, None, None, None),
            P(band, None),
            P(band, None),
            P(band),
        ),
        out_specs=(P("tm", ("z_lo", "x"), band, None), P("tm", band, ("z_lo", "x"), None, None)),
        check_vma=False,
    )
```

```python
import functools
import math

import jax
import jax.numpy as jnp
from jax import lax
from jax.experimental import pallas as pl
from jax.experimental.pallas import tpu as pltpu
from jax.sharding import Mesh, PartitionSpec as P

EXTENT = 64
Z_LO = 4
CORES = 2


def gram_kernel(
    base_ref, mom_hbm, evecs_hbm, out_ref, evecs_ref, right_ref, mom_ref, evecs_sems, mom_sem
):
    tcount, _, colours, sites, nvec = evecs_ref.shape
    n_x = out_ref.shape[0] // tcount
    n_zl, rows = out_ref.shape[1:3]
    mom_copy = pltpu.make_async_copy(mom_hbm, mom_ref, mom_sem)
    mom_copy.start()
    loads = [
        pltpu.make_async_copy(evecs_hbm.at[t], evecs_ref.at[t], evecs_sems.at[t]) for t in range(tcount)
    ]
    for copy in loads:
        copy.start()
    site = base_ref[0] + lax.broadcasted_iota(jnp.int32, (sites, nvec), 0)
    xs = site & (EXTENT - 1)
    ys = (site >> 6) & (EXTENT - 1)
    zs = site >> 12
    mom_copy.wait()
    wave = (mom_ref[0, 0] * xs + mom_ref[0, 1] * ys + mom_ref[0, 2] * zs) & (EXTENT - 1)
    theta = wave.astype(jnp.float32) * jnp.float32(2.0 * math.pi / EXTENT)
    cosine = jnp.cos(theta)
    sine = jnp.sin(theta)

    def rotate(t):
        for colour in range(colours):
            vreal = evecs_ref[t, 0, colour].astype(jnp.float32)
            vimag = evecs_ref[t, 1, colour].astype(jnp.float32)
            right_ref[t, colour, :, :nvec] = (cosine * vreal + sine * vimag).astype(jnp.bfloat16)
            right_ref[t, colour, :, nvec:] = (cosine * vimag - sine * vreal).astype(jnp.bfloat16)

    def multiply(t):
        right = right_ref[t].reshape(colours * sites, 2 * nvec)
        with_real, with_imag = (
            lax.dot_general(
                evecs_ref[t, part].reshape(colours * sites, nvec),
                right,
                (((0,), (0,)), ((), ())),
                preferred_element_type=jnp.float32,
            )
            for part in range(2)
        )
        meson = jnp.concatenate(
            [with_real[:, :nvec] + with_imag[:, nvec:], with_real[:, nvec:] - with_imag[:, :nvec]], axis=1
        ).astype(out_ref.dtype)
        for x in range(n_x):
            for zl in range(n_zl):
                first = (zl * n_x + x) * rows
                out_ref[x * tcount + t, zl] = meson[first : first + rows]

    groups = [list(range(4)), list(range(4, 8))]
    for g, group in enumerate(groups):
        for t in group:
            loads[t].wait()
        for t in group:
            rotate(t)
            multiply(t)


def sum_kernel(parts_ref, out_hbm, total_ref, sems):
    copies = []
    for zl in range(total_ref.shape[0]):
        total_ref[zl] = jnp.sum(parts_ref[:, zl].astype(jnp.float32), axis=0).astype(jnp.bfloat16)
        for band in range(out_hbm.shape[0]):
            copies.append(pltpu.make_async_copy(total_ref.at[zl], out_hbm.at[band, zl], sems.at[band, zl]))
            copies[-1].start()
    for copy in copies:
        copy.wait()


def pick_kernel(counts_ref, pairs_hbm, peram_hbm, out_ref, pairs_ref, pairs_sem, sems):
    nvec = peram_hbm.shape[-1]
    pairs_copy = pltpu.make_async_copy(pairs_hbm, pairs_ref, pairs_sem)
    pairs_copy.start()
    pairs_copy.wait()
    copies = [
        pltpu.make_async_copy(
            peram_hbm.at[pairs_ref[0, c]], out_ref.at[c // 2, :, :, pl.ds(c % 2 * nvec, nvec)], sems.at[c]
        )
        for c in range(pairs_ref.shape[1])
    ]
    for copy in copies:
        copy.start()
    for c, copy in enumerate(copies):
        copy.wait()

        @pl.when(c >= counts_ref[0])
        def _():
            out_ref[c // 2, :, :, c % 2 * nvec : (c % 2 + 1) * nvec] = jnp.zeros((2, nvec, nvec), out_ref.dtype)


def block_kernel(band_ref, parts_ref, chosen_ref, meson_hbm, out_hbm, total_ref, meson_ref, out_ref, sems):
    n_zh, cores, _, rows, width = parts_ref.shape
    moms = cores * n_zh
    slots = out_ref.shape[0]
    size = moms * rows
    nvec = width // 2
    for core in range(cores):
        for zh in range(n_zh):
            total_ref[zh * cores + core] = jnp.sum(parts_ref[zh, core].astype(jnp.float32), axis=0)
    own = total_ref[band_ref[0]]
    for row in range(rows):
        meson_ref[row] = own[row : row + 1]
    meson_copy = pltpu.make_async_copy(meson_ref, meson_hbm, sems.at[slots])
    meson_copy.start()
    left = jnp.swapaxes(total_ref[...], 0, 1).reshape(size, width)
    mreal = left[:, :nvec]
    mimag = left[:, nvec:]
    both = jnp.concatenate(
        [jnp.concatenate([mreal, -mimag], axis=1), jnp.concatenate([mimag, mreal], axis=1)], axis=0
    ).astype(jnp.bfloat16)
    copies = [meson_copy]
    for pair in range(slots // 2):
        right = chosen_ref[pair].reshape(width, 2 * nvec)
        prods = jnp.dot(both, right, preferred_element_type=jnp.float32)
        for q in range(2):
            c = 2 * pair + q
            prod = prods[:, q * nvec : (q + 1) * nvec]
            out_ref[c, :, :, :nvec] = prod[:size].reshape(rows, moms, nvec)
            out_ref[c, :, :, nvec:] = prod[size:].reshape(rows, moms, nvec)
            copies.append(pltpu.make_async_copy(out_ref.at[c], out_hbm.at[c], sems.at[c]))
            copies[-1].start()
    for copy in copies:
        copy.wait()


def per_device(evecs, peram, mom, pairs, counts):
    tcount, _, colours, piece_len, nvec = evecs.shape
    n_tm = lax.axis_size("tm")
    n_zl = lax.axis_size("z_lo")
    n_x = lax.axis_size("x")
    n_zh = lax.axis_size("z_hi")
    n_core = lax.axis_size("core")
    n_band = n_zh * n_core
    slots = pairs.shape[1]
    rows = nvec // (n_zl * n_x)
    width = 2 * nvec
    place = (lax.axis_index("tm") * n_zl + lax.axis_index("z_lo")) * n_x + lax.axis_index("x")
    base = (place * piece_len).astype(jnp.int32)
    hold = functools.partial(pltpu.with_memory_space_constraint, memory_space=pltpu.HBM)
    smem = pl.BlockSpec(memory_space=pltpu.SMEM)
    vmem = pl.BlockSpec(memory_space=pltpu.VMEM)
    hbm = pl.BlockSpec(memory_space=pltpu.HBM)
    parts = pl.pallas_call(
        gram_kernel,
        in_specs=[smem, hbm, hbm],
        out_specs=vmem,
        out_shape=jax.ShapeDtypeStruct((n_tm * n_x, n_zl, rows, width), jnp.bfloat16),
        scratch_shapes=[
            pltpu.VMEM((tcount, 2, colours, piece_len, nvec), jnp.bfloat16),
            pltpu.VMEM((tcount, colours, piece_len, width), jnp.bfloat16),
            pltpu.SMEM(mom.shape, jnp.int32),
            pltpu.SemaphoreType.DMA((tcount,)),
            pltpu.SemaphoreType.DMA,
        ],
        compiler_params=pltpu.CompilerParams(vmem_limit_bytes=16 << 20),
        name="gram",
    )(base.reshape(1), hold(mom), hold(evecs))
    parts = parts.reshape(n_tm * n_x, n_zl * rows, width)
    parts = lax.all_to_all(parts, ("x", "tm"), 0, 0, tiled=True)
    parts = parts.reshape(n_tm * n_x, n_zl, rows, width)
    parts = pl.pallas_call(
        sum_kernel,
        in_specs=[vmem],
        out_specs=hbm,
        out_shape=jax.ShapeDtypeStruct((n_band, n_zl, rows, width), jnp.bfloat16),
        scratch_shapes=[pltpu.VMEM((n_zl, rows, width), jnp.bfloat16), pltpu.SemaphoreType.DMA((n_band, n_zl))],
        compiler_params=pltpu.CompilerParams(vmem_limit_bytes=8 << 20),
        name="total",
    )(parts)
    parts = parts.reshape(n_band * n_zl, rows, width)
    parts = lax.all_to_all(parts, ("z_hi", "core", "z_lo"), 0, 0, tiled=True)
    chosen = pl.pallas_call(
        pick_kernel,
        in_specs=[smem, hbm, hbm],
        out_specs=vmem,
        out_shape=jax.ShapeDtypeStruct((slots // 2, 2, nvec, 2 * nvec), jnp.bfloat16),
        scratch_shapes=[
            pltpu.SMEM(pairs.shape, jnp.int32),
            pltpu.SemaphoreType.DMA,
            pltpu.SemaphoreType.DMA((slots,)),
        ],
        compiler_params=pltpu.CompilerParams(vmem_limit_bytes=8 << 20),
        cost_estimate=pl.CostEstimate(flops=0, transcendentals=0, bytes_accessed=8 * slots * nvec * nvec),
        name="pick",
    )(counts, hold(pairs), hold(peram[0]))
    meson, blocks = pl.pallas_call(
        block_kernel,
        in_specs=[smem, vmem, vmem],
        out_specs=[hbm, hbm],
        out_shape=[
            jax.ShapeDtypeStruct((rows, 1, width), jnp.float32),
            jax.ShapeDtypeStruct((slots, rows, n_band, width), jnp.float32),
        ],
        scratch_shapes=[
            pltpu.VMEM((n_band, rows, width), jnp.float32),
            pltpu.VMEM((rows, 1, width), jnp.float32),
            pltpu.VMEM((slots, rows, n_band, width), jnp.float32),
            pltpu.SemaphoreType.DMA((slots + 1,)),
        ],
        compiler_params=pltpu.CompilerParams(vmem_limit_bytes=8 << 20),
        name="blocks",
    )(
        (lax.axis_index("z_hi") * n_core + lax.axis_index("core")).astype(jnp.int32).reshape(1),
        parts.reshape(n_zh, n_core, n_zl, rows, width),
        chosen,
    )
    return meson[None], blocks[None]


def solution(mesh):
    n_tm, n_band, n_space = (mesh.shape[name] for name in ("tm", "band", "space"))
    fine = Mesh(
        mesh.devices.reshape(n_tm, n_band // CORES, CORES, Z_LO, n_space // Z_LO),
        ("tm", "z_hi", "core", "z_lo", "x"),
    )
    band = ("z_hi", "core")
    return jax.shard_map(
        per_device,
        mesh=fine,
        in_specs=(
            P(None, None, None, ("tm", "z_lo", "x"), None),
            P("tm", None, None, None, None),
            P(band, None),
            P(band, None),
            P(band),
        ),
        out_specs=(P("tm", ("z_lo", "x"), band, None), P("tm", band, ("z_lo", "x"), None, None)),
        check_vma=False,
    )
```
